256 devices in a mesh: row: 16 (over x_lo, z), col: 16 (over x_hi, y, core).
Axes of the slice: x: 4 (x_hi: 2, x_lo: 2; x = x_hi * 2 + x_lo), y: 4, z: 8, core: 2. Of those that a mesh axis runs over, the one named last changes fastest.
Arguments:
- features: bfloat16 [32768, 1024], P(('row', 'col')), may hold values from -6 to 6
- weight: bfloat16 [1024, 1024], replicated, may hold values from -0.1875 to 0.1875
- cotangent: bfloat16 [32768, 1024], P(('col', 'row')), may hold values from -6 to 6
- tile_values: bfloat16 [16, 16, 64, 128, 128], P('row', 'col'), may hold values from -0.1875 to 0.1875
- block_row: int32 [16, 16, 64], P('row', 'col'), may hold values from 0 to 15, as said below
- block_column: int32 [16, 16, 64], P('row', 'col'), may hold values from 0 to 15, as said below
- tile_count: int32 [16, 16], P('row', 'col'), may hold values from 16 to 64, as said below
Outputs:
- activated: bfloat16 [32768, 1024], P(('col', 'row'))
- feat_grad: bfloat16 [32768, 1024], P(('row', 'col'))
- weight_grad: float32 [1024, 1024], replicated
The draws below stay inside these ranges and needn't reach their ends.
Inputs may be any that keep to these rules, and one draw needn't show every extreme that they name: `block_row`: within one grid position the slots name distinct region cells. `block_column`: within one grid position the slots name distinct region cells. `tile_count`: some grid position has exactly 64 live slots.
All inputs are finite; a program needn't handle non-finite values.
Results may differ from the reference program's by a relative error of at most 0.02.
Values may be sent and summed in bfloat16 or wider, within the bound.
A program may use at most 128 MiB of HBM per device.

```python
import jax
import jax.numpy as jnp
from jax import lax

F = 1024
BLK = 128
RB_DEV = 1
NODES = 32768
REGION_ROWS = 16
REGION_COLS = 16
TILES = 64
N_ROW = 16
N_COL = 16


def region_cells(key):
    keys = jax.random.split(jax.random.fold_in(key, 11), N_ROW * N_COL)

    def pick_cells(single):
        return jax.random.permutation(single, REGION_ROWS * REGION_COLS)[:TILES]
    cells = jax.vmap(pick_cells)(keys).astype(jnp.int32)
    return cells.reshape(N_ROW, N_COL, TILES)


def draw_block_row(key, part):
    return region_cells(key) // REGION_COLS


def draw_block_column(key, part):
    return region_cells(key) % REGION_COLS


def draw_tile_count(key, part):
    counts = jax.random.randint(jax.random.fold_in(key, 5), (N_ROW * N_COL,), TILES // 4, TILES + 1)
    chosen = jax.random.randint(jax.random.fold_in(key, 7), (), 0, N_ROW * N_COL)
    places = jnp.arange(N_ROW * N_COL, dtype=jnp.int32)
    counts = jnp.where(places == chosen, TILES, counts)
    return counts.astype(jnp.int32).reshape(N_ROW, N_COL)


def shard_levels(own_key, dims, cuts, smallest, top_value):
    def one(axis_at, shards_of):
        heights = jax.random.uniform(jax.random.fold_in(jax.random.fold_in(own_key, 6), axis_at), (shards_of,), jnp.float32, smallest / len(cuts), top_value / len(cuts))
        return jnp.repeat(jnp.exp(heights), dims[axis_at] // shards_of).reshape((-1,) + (1,) * (len(dims) - axis_at - 1))

    factor_of = one(*cuts[0])
    for cut in cuts[1:]:
        factor_of = factor_of * one(*cut)
    return factor_of


def centred(stream_key, shape, scale, most, cuts=(), held_as=jnp.bfloat16):
    gain = shard_levels(stream_key, shape, cuts, -0.22, 0.18) if cuts else 1.0
    drawn = jax.random.normal(stream_key, shape, jnp.float32) * scale * gain
    return jnp.minimum(jnp.maximum(drawn, -most), most).astype(held_as)


def setup_inputs(seed: int = 0) -> dict:
    key_list = jax.random.split(jax.random.key(seed), 8)
    features = centred(key_list[0], (NODES, F), 1.0, 6.0, ((0, 256),))
    weight = centred(key_list[1], (F, F), F ** -0.5, 0.1875)
    cotangent = centred(key_list[2], (NODES, F), 1.0, 6.0, ((0, 256),))
    tile_values = centred(key_list[3], (N_ROW, N_COL, TILES, BLK, BLK), (1.2 * (TILES * BLK // RB_DEV) ** -0.5), 0.1875, ((0, 16), (1, 16)))
    block_row = draw_block_row(jax.random.fold_in(key_list[7], 71), 0)
    block_column = draw_block_column(jax.random.fold_in(key_list[7], 71), 0)
    tile_count = draw_tile_count(jax.random.fold_in(key_list[7], 71), 0)
    return dict(features=features, weight=weight, cotangent=cotangent, tile_values=tile_values, block_row=block_row, block_column=block_column, tile_count=tile_count)


def silu_slope(hidden):
    sigmoid = jax.nn.sigmoid(hidden)
    return sigmoid * (1.0 + hidden * (1.0 - sigmoid))


def spread_tiles(source, tile_block, index_in, index_out, is_live, out_blocks, flipped):
    blocks = source.reshape(-1, BLK, F).astype(jnp.float32)
    picked = blocks[index_in]
    matrix = tile_block.astype(jnp.float32)
    form = "tba,tbf->taf" if flipped else "tab,tbf->taf"
    products = jnp.einsum(form, matrix, picked, precision=lax.Precision.HIGHEST)
    products = products * is_live.astype(jnp.float32)[:, None, None]
    summed = jax.ops.segment_sum(products, index_out, num_segments=out_blocks)
    return summed.reshape(out_blocks * BLK, F)


def reference(features, weight, cotangent, tile_values, block_row, block_column, tile_count):
    span = BLK * RB_DEV
    projected = jnp.dot(features, weight, preferred_element_type=jnp.float32).astype(jnp.bfloat16)
    slots = jnp.arange(TILES, dtype=jnp.int32)

    def forward_group(column):
        def add_row(grid_row, accum):
            first = (grid_row * (N_COL * span)).astype(jnp.int32)
            source = lax.dynamic_slice_in_dim(projected, first, N_COL * span, 0)
            is_live = slots < tile_count[grid_row, column]
            part = spread_tiles(source, tile_values[grid_row, column], block_column[grid_row, column],
                                block_row[grid_row, column], is_live, REGION_ROWS, False)
            return accum + lax.optimization_barrier(part.astype(jnp.bfloat16)).astype(jnp.float32)
        return lax.fori_loop(0, N_ROW, add_row, jnp.zeros((N_ROW * span, F), jnp.float32))

    hidden = lax.map(forward_group, jnp.arange(N_COL, dtype=jnp.int32)).reshape(NODES, F)
    activated = jax.nn.silu(hidden).astype(jnp.bfloat16)
    hidden_grad = (cotangent.astype(jnp.float32) * silu_slope(hidden)).astype(jnp.bfloat16)

    def backward_group(grid_row):
        def add_column(column, accum):
            first = (column * (N_ROW * span)).astype(jnp.int32)
            source = lax.dynamic_slice_in_dim(hidden_grad, first, N_ROW * span, 0)
            is_live = slots < tile_count[grid_row, column]
            part = spread_tiles(source, tile_values[grid_row, column], block_row[grid_row, column],
                                block_column[grid_row, column], is_live, REGION_COLS, True)
            return accum + lax.optimization_barrier(part.astype(jnp.bfloat16)).astype(jnp.float32)
        return lax.fori_loop(0, N_COL, add_column, jnp.zeros((N_COL * span, F), jnp.float32))

    feat_delta = lax.map(backward_group, jnp.arange(N_ROW, dtype=jnp.int32)).reshape(NODES, F).astype(jnp.bfloat16)
    feat_grad = jnp.dot(feat_delta, weight.T, preferred_element_type=jnp.float32).astype(jnp.bfloat16)
    weight_grad = jnp.dot(features.T, feat_delta, preferred_element_type=jnp.float32) * (NODES ** -0.5)
    return activated, feat_grad, weight_grad
```

```python
import jax
import jax.numpy as jnp
from jax import lax
from jax.experimental import pallas as pl
from jax.experimental.pallas import tpu as pltpu
from jax.sharding import PartitionSpec as P

MESH = pl.DeviceIdType.MESH
BF = jnp.bfloat16
F32 = jnp.float32
NZ = 8
NY = 4
BLK = 128
HALF = 512


def remote(src, dst, send, recv, device):
    return pltpu.make_async_remote_copy(
        src_ref=src, dst_ref=dst, send_sem=send, recv_sem=recv,
        device_id=device, device_id_type=MESH,
    )


def kernel(
    slot_of, feat, weight, cot, tiles_in,
    act, fgrad, wgrad,
    xg, proj, hg, tiles, tiles_t, strip, part,
    rr, rrx, rc, rcs, rcr, rcx, dp, dg, ws, wr, wxs, wxr, zg,
    tile_sem,
    a_ys, a_yr, a_xs, a_xr, a_ds, a_dr,
    b_s, b_r, bx_s, bx_r,
    c_s, c_r, cx_s, cx_r,
    e_s, e_r, ex_s, ex_r, ed_s, ed_r,
    t_s, t_r, z_s, z_r, zx_s, zx_r, g_s, g_r,
    w_ys, w_yr, w_xs, w_xr, w_ds, w_dr,
):
    row = lax.axis_index("row")
    col = lax.axis_index("col")
    xl, z = row // NZ, row % NZ
    xh, y, core = col // 8, (col // 2) % NY, col % 2

    def z_dev(k):
        return (xl * NZ + (z + k + NZ) % NZ, col)

    def y_dev(d):
        return (row, xh * 8 + ((y + 1 - 2 * d + NY) % NY) * 2 + core)

    xl_dev = ((1 - xl) * NZ + z, col)
    xh_dev = (row, (1 - xh) * 8 + y * 2 + core)
    sib_dev = (row, xh * 8 + y * 2 + 1 - core)

    load_tiles = pltpu.make_async_copy(tiles_in, tiles.at[pl.ds(0, 64)], tile_sem)
    load_tiles.start()

    barrier = pltpu.get_barrier_semaphore()
    for k in range(1, 16):
        pl.semaphore_signal(barrier, inc=1, device_id=(row, (col + k) % 16), device_id_type=MESH)
    for k in range(1, NZ):
        pl.semaphore_signal(barrier, inc=1, device_id=z_dev(k), device_id_type=MESH)
    pl.semaphore_signal(barrier, inc=1, device_id=xl_dev, device_id_type=MESH)
    pl.semaphore_wait(barrier, 15 + NZ - 1 + 1)

    def gather_col(own, slot, ys, yr, xs, xr, ds, dr):
        def source(d, sub, s, other):
            yy = (y + (2 * d - 1) * s + NY) % NY
            xx = xh if sub == 1 else 1 - xh
            return xx * 8 + yy * 2 + (1 - core if other else core)

        def send_y(d, sub, s):
            here = slot(source(d, sub, s, False), d)
            there = here
            src = own(d) if (sub == 1 and s == 0) else here
            return remote(src, there, ys.at[d, sub, s], yr.at[d, sub, s], y_dev(d))

        def send_d(d, sub, s):
            here = slot(source(d, sub, s, False), d)
            src = own(d) if (sub == 1 and s == 0) else here
            return remote(src, here, ds.at[d, sub, s], dr.at[d, sub, s], sib_dev)

        def send_x(d):
            return remote(own(d), slot(col, d), xs.at[d], xr.at[d], xh_dev)

        def got(d, sub, s):
            here = slot(source(d, sub, s, False), d)
            remote(here, here, ys.at[d, sub, s - 1], yr.at[d, sub, s - 1], y_dev(d)).wait_recv()

        def arrive(sub, s):
            for d in range(2):
                got(d, sub, s)
                if s < NY - 1:
                    send_y(d, sub, s).start()
                send_d(d, sub, s).start()

        def start():
            for d in range(2):
                send_y(d, 1, 0).start()
                send_x(d).start()
                send_d(d, 1, 0).start()

        def go():
            arrive(1, 1)
            for d in range(2):
                here = slot(source(d, 0, 0, False), d)
                remote(here, here, xs.at[d], xr.at[d], xh_dev).wait_recv()
                send_y(d, 0, 0).start()
                send_d(d, 0, 0).start()
            arrive(1, 2)
            arrive(0, 1)
            arrive(1, 3)
            arrive(0, 2)
            arrive(0, 3)
            for sub in (1, 0):
                for s in range(NY):
                    for d in range(2):
                        here = slot(source(d, sub, s, True), d)
                        remote(here, here, ds.at[d, sub, s], dr.at[d, sub, s], sib_dev).wait_recv()

        def drain():
            for d in range(2):
                send_x(d).wait_send()
                for sub in range(2):
                    for s in range(NY):
                        if s < NY - 1:
                            send_y(d, sub, s).wait_send()
                        send_d(d, sub, s).wait_send()

        return start, go, drain

    def feat_half(d):
        return feat.at[pl.ds(64 * d, 64)]

    def xg_slot(c, d):
        return xg.at[pl.ds(pl.multiple_of(c * BLK + 64 * d, 64), 64)]

    fa_start, fa_go, fa_drain = gather_col(feat_half, xg_slot, a_ys, a_yr, a_xs, a_xr, a_ds, a_dr)
    fa_start()
    xg[pl.ds(pl.multiple_of(col * BLK, BLK), BLK), :] = feat[...]
    load_tiles.wait()
    tiles[64] = jnp.zeros((BLK, BLK), BF)
    tiles_t[64] = jnp.zeros((BLK, BLK), BF)

    def flip(t, carry):
        tiles_t[t] = tiles[t].T
        return carry

    lax.fori_loop(0, 64, flip, 0)
    fa_go()

    def project(b, carry):
        rows = pl.ds(pl.multiple_of(b * 256, 256), 256)
        value = jnp.dot(xg[rows, :], weight[...], preferred_element_type=F32).astype(BF)
        proj[0, rows, :] = value[:, :HALF]
        proj[1, rows, :] = value[:, HALF:]
        return carry

    lax.fori_loop(0, 8, project, 0)

    def product(source, table, first, step, base, d):
        for i in range(16):
            strip[:, i * BLK:(i + 1) * BLK] = table[slot_of[first + i * step]]
        return jnp.dot(strip[...], source[d], preferred_element_type=F32)

    def rr_send(q, d, s):
        return remote(rr.at[q, s], rr.at[q, s + 1], b_s.at[q, s], b_r.at[q, s], z_dev(1 - 2 * d))

    def rrx_send(d):
        return remote(rr.at[2 * d, NZ - 1], rrx.at[d], bx_s.at[d], bx_r.at[d], xl_dev)

    def row_step(s, carry):
        def compute(q, inner):
            d, sub = q // 2, q % 2
            zd = (z + (2 * d - 1) * (s + 1) + NZ) % NZ
            xd = xl + (1 - sub) * (1 - 2 * xl)
            part[q] = product(proj, tiles, (xd * NZ + zd) * 16, 1, 0, d)
            return inner

        lax.fori_loop(0, 4, compute, 0)

        def pass_on(q, inner):
            d, sub = q // 2, q % 2

            @pl.when(s > 0)
            def _():
                remote(rr.at[q, s], rr.at[q, s], b_s.at[q, s - 1], b_r.at[q, s - 1],
                       z_dev(1 - 2 * d)).wait_recv()
                part[q] = part[q] + rr[q, s].astype(F32)

            rr[q, s] = part[q].astype(BF)

            @pl.when(s < NZ - 1)
            def _():
                rr_send(q, d, s).start()

            @pl.when((s == NZ - 1) & (sub == 0))
            def _():
                rrx_send(d).start()

            return inner

        lax.fori_loop(0, 4, pass_on, 0)
        return carry

    lax.fori_loop(0, NZ, row_step, 0)

    own_h = pl.ds(pl.multiple_of(row * BLK, BLK), BLK)
    for d in range(2):
        remote(rrx.at[d], rrx.at[d], bx_s.at[d], bx_r.at[d], xl_dev).wait_recv()
        lanes = slice(d * HALF, (d + 1) * HALF)
        hidden = part[2 * d + 1] + rrx[d].astype(F32)
        sig = 1.0 / (1.0 + jnp.exp(-hidden))
        act[:, lanes] = (hidden * sig).astype(BF)
        slope = sig * (1.0 + hidden * (1.0 - sig))
        hg[d, own_h, :] = (cot[:, lanes].astype(F32) * slope).astype(BF)

    def hg_at(d, sub, s):
        zz = (z + (2 * d - 1) * s + NZ) % NZ
        xx = xl if sub == 1 else 1 - xl
        return hg.at[d, pl.ds(pl.multiple_of((xx * NZ + zz) * BLK, BLK), BLK)]

    def ag_send(d, sub, s):
        here = hg_at(d, sub, s)
        return remote(here, here, c_s.at[d, sub, s], c_r.at[d, sub, s], z_dev(1 - 2 * d))

    def agx_send(d):
        here = hg_at(d, 1, 0)
        return remote(here, here, cx_s.at[d], cx_r.at[d], xl_dev)

    def ag_arrive(sub, s):
        for d in range(2):
            here = hg_at(d, sub, s)
            remote(here, here, c_s.at[d, sub, s - 1], c_r.at[d, sub, s - 1],
                   z_dev(1 - 2 * d)).wait_recv()
            if s < NZ - 1:
                ag_send(d, sub, s).start()

    for d in range(2):
        ag_send(d, 1, 0).start()
        agx_send(d).start()
    for d in range(2):
        here = hg_at(d, 0, 0)
        remote(here, here, cx_s.at[d], cx_r.at[d], xl_dev).wait_recv()
        ag_send(d, 0, 0).start()
    for s in range(1, NZ):
        ag_arrive(1, s)
        ag_arrive(0, s)

    def sib_send(q, s):
        return remote(rcs.at[q, s], rcr.at[q, s], ed_s.at[q, s], ed_r.at[q, s], sib_dev)

    def rc_send(q, d, s):
        return remote(rc.at[q, s], rc.at[q, s + 1], e_s.at[q, s], e_r.at[q, s], y_dev(d))

    def rcx_send(d):
        return remote(rc.at[2 * d, NY - 1], rcx.at[d], ex_s.at[d], ex_r.at[d], xh_dev)

    def col_step(s, carry):
        def place(q):
            d, sub = q // 2, q % 2
            yd = (y + (2 * d - 1) * (s + 1) + NY) % NY
            xd = xh + (1 - sub) * (1 - 2 * xh)
            return d, xd * 8 + yd * 2

        def compute_other(q, inner):
            d, base = place(q)
            rcs[q, s] = product(hg, tiles_t, base + 1 - core, 16, 0, d).astype(BF)
            sib_send(q, s).start()
            return inner

        def compute_own(q, inner):
            d, base = place(q)
            part[q] = product(hg, tiles_t, base + core, 16, 0, d)
            return inner

        lax.fori_loop(0, 4, compute_other, 0)
        lax.fori_loop(0, 4, compute_own, 0)

        def pass_on(q, inner):
            d, sub = q // 2, q % 2
            remote(rcr.at[q, s], rcr.at[q, s], ed_s.at[q, s], ed_r.at[q, s], sib_dev).wait_recv()
            part[q] = part[q] + rcr[q, s].astype(F32)

            @pl.when(s > 0)
            def _():
                remote(rc.at[q, s], rc.at[q, s], e_s.at[q, s - 1], e_r.at[q, s - 1],
                       y_dev(d)).wait_recv()
                part[q] = part[q] + rc[q, s].astype(F32)

            rc[q, s] = part[q].astype(BF)

            @pl.when(s < NY - 1)
            def _():
                rc_send(q, d, s).start()

            @pl.when((s == NY - 1) & (sub == 0))
            def _():
                rcx_send(d).start()

            return inner

        lax.fori_loop(0, 4, pass_on, 0)
        return carry

    lax.fori_loop(0, NY, col_step, 0)

    for d in range(2):
        remote(rcx.at[d], rcx.at[d], ex_s.at[d], ex_r.at[d], xh_dev).wait_recv()
        delta = (part[2 * d + 1] + rcx[d].astype(F32)).astype(BF)
        for k in range(4):
            dp[4 * d + k] = delta[:, k * BLK:(k + 1) * BLK]

    def piece_send(k):
        peer = (col + k) % 16
        return remote(dp.at[peer // 2], dg.at[col], t_s.at[k], t_r.at[k], (row, peer))

    for k in range(1, 16):
        piece_send(k).start()
    dg[col] = dp[col // 2]

    delta = jnp.concatenate([dp[k] for k in range(8)], axis=1)
    fgrad[...] = lax.dot_general(
        delta, weight[...], (((1,), (1,)), ((), ())), preferred_element_type=F32
    ).astype(BF)

    for k in range(1, 16):
        there = dg.at[(col - k + 16) % 16]
        remote(there, there, t_s.at[k], t_r.at[k], (row, (col + k) % 16)).wait_recv()
    for i in range(16):
        strip[:, i * BLK:(i + 1) * BLK] = dg[i].T
    lanes = pl.ds(pl.multiple_of(core * HALF, HALF), HALF)
    terms = jnp.dot(strip[...], xg[:, lanes], preferred_element_type=F32).T
    for k in range(NZ):
        ws[k] = terms[k * 64:(k + 1) * 64, :].astype(BF)

    def zsum_send(k):
        return remote(ws.at[(z + k) % NZ], wr.at[z], z_s.at[k], z_r.at[k], z_dev(k))

    for k in range(1, NZ):
        zsum_send(k).start()
    total = ws[z].astype(F32)
    for k in range(1, NZ):
        zz = (z - k + NZ) % NZ
        remote(wr.at[zz], wr.at[zz], z_s.at[k], z_r.at[k], z_dev(k)).wait_recv()
        total = total + wr[zz].astype(F32)
    wxs[...] = total.astype(BF)
    wx_send = remote(wxs, wxr, zx_s, zx_r, xl_dev)
    wx_send.start()
    wx_send.wait_recv()
    zg[pl.ds(pl.multiple_of(z * 64, 64), 64), :] = (wxs[...].astype(F32) + wxr[...].astype(F32)).astype(BF)

    def zg_at(k):
        return zg.at[pl.ds(pl.multiple_of(((z + k + NZ) % NZ) * 64, 64), 64)]

    def zg_send(k):
        return remote(zg_at(0), zg_at(0), g_s.at[k], g_r.at[k], z_dev(k))

    for k in range(1, NZ):
        zg_send(k).start()
    for k in range(1, NZ):
        remote(zg_at(-k), zg_at(-k), g_s.at[k], g_r.at[k], z_dev(k)).wait_recv()

    def zg_half(d):
        return zg.at[pl.ds(256 * d, 256)]

    def wgrad_slot(c, d):
        return wgrad.at[c, pl.ds(256 * d, 256)]

    wa_start, wa_go, wa_drain = gather_col(zg_half, wgrad_slot, w_ys, w_yr, w_xs, w_xr, w_ds, w_dr)
    wa_start()
    wgrad[col] = zg[...]
    wa_go()

    fa_drain()
    wa_drain()
    for d in range(2):
        rrx_send(d).wait_send()
        agx_send(d).wait_send()
        rcx_send(d).wait_send()
        for sub in range(2):
            q = 2 * d + sub
            for s in range(NZ - 1):
                rr_send(q, d, s).wait_send()
                ag_send(d, sub, s).wait_send()
            for s in range(NY - 1):
                rc_send(q, d, s).wait_send()
            for s in range(NY):
                sib_send(q, s).wait_send()
    for k in range(1, 16):
        piece_send(k).wait_send()
    for k in range(1, NZ):
        zsum_send(k).wait_send()
        zg_send(k).wait_send()
    wx_send.wait_send()


def layer(slot_of, features, weight, cotangent, tiles):
    vmem = pl.BlockSpec(memory_space=pltpu.VMEM)
    dma = pltpu.SemaphoreType.DMA
    gather_sems = [dma((2, 2, 3)), dma((2, 2, 3)), dma((2,)), dma((2,)), dma((2, 2, 4)), dma((2, 2, 4))]
    return pl.pallas_call(
        kernel,
        name="layer",
        out_shape=(
            jax.ShapeDtypeStruct((BLK, 1024), BF),
            jax.ShapeDtypeStruct((BLK, 1024), BF),
            jax.ShapeDtypeStruct((16, HALF, BLK), BF),
        ),
        in_specs=[
            pl.BlockSpec(memory_space=pltpu.SMEM), vmem, vmem, vmem,
            pl.BlockSpec(memory_space=pl.ANY),
        ],
        out_specs=(vmem, vmem, vmem),
        scratch_shapes=[
            pltpu.VMEM((2048, 1024), BF),
            pltpu.VMEM((2, 2048, HALF), BF),
            pltpu.VMEM((2, 2048, HALF), BF),
            pltpu.VMEM((65, BLK, BLK), BF),
            pltpu.VMEM((65, BLK, BLK), BF),
            pltpu.VMEM((BLK, 2048), BF),
            pltpu.VMEM((4, BLK, HALF), F32),
            pltpu.VMEM((4, NZ, BLK, HALF), BF),
            pltpu.VMEM((2, BLK, HALF), BF),
            pltpu.VMEM((4, NY, BLK, HALF), BF),
            pltpu.VMEM((4, NY, BLK, HALF), BF),
            pltpu.VMEM((4, NY, BLK, HALF), BF),
            pltpu.VMEM((2, BLK, HALF), BF),
            pltpu.VMEM((8, BLK, BLK), BF),
            pltpu.VMEM((16, BLK, BLK), BF),
            pltpu.VMEM((NZ, 64, BLK), BF),
            pltpu.VMEM((NZ, 64, BLK), BF),
            pltpu.VMEM((64, BLK), BF),
            pltpu.VMEM((64, BLK), BF),
            pltpu.VMEM((HALF, BLK), BF),
            dma,
            *gather_sems,
            dma((4, 7)), dma((4, 7)), dma((2,)), dma((2,)),
            dma((2, 2, 7)), dma((2, 2, 7)), dma((2,)), dma((2,)),
            dma((4, 3)), dma((4, 3)), dma((2,)), dma((2,)), dma((4, 4)), dma((4, 4)),
            dma((16,)), dma((16,)), dma((NZ,)), dma((NZ,)), dma, dma, dma((NZ,)), dma((NZ,)),
            *gather_sems,
        ],
        compiler_params=pltpu.CompilerParams(
            collective_id=0, has_side_effects=True, vmem_limit_bytes=60 * 1024 * 1024,
        ),
    )(slot_of, features, weight, cotangent, tiles)


def on_device(features, weight, cotangent, tile_values, block_row, block_column, tile_count):
    slots = jnp.arange(64, dtype=jnp.int32)
    cell = block_row[0, 0] * 16 + block_column[0, 0]
    cell = jnp.where(slots < tile_count[0, 0], cell, -1)
    named = cell[None, :] == jnp.arange(256, dtype=jnp.int32)[:, None]
    slot_of = jnp.min(jnp.where(named, slots[None, :], 64), axis=1)
    activated, feat_grad, pieces = layer(slot_of, features, weight, cotangent, tile_values[0, 0])
    pieces = pieces.reshape(8, 2, HALF, BLK).transpose(1, 2, 0, 3).reshape(1024, 1024)
    weight_grad = pieces.astype(F32) * 32768 ** (-0.5)
    return activated, feat_grad, weight_grad


def solution(mesh):
    return jax.shard_map(
        on_device,
        mesh=mesh,
        in_specs=(
            P(("row", "col"), None),
            P(),
            P(("col", "row"), None),
            P("row", "col", None, None, None),
            P("row", "col", None),
            P("row", "col", None),
            P("row", "col"),
        ),
        out_specs=(P(("col", "row"), None), P(("row", "col"), None), P()),
        check_vma=False,
    )
```

```python
import jax
import jax.numpy as jnp
from jax import lax
from jax.experimental import pallas as pl
from jax.experimental.pallas import tpu as pltpu
from jax.sharding import PartitionSpec as P

MESH = pl.DeviceIdType.MESH
BF = jnp.bfloat16
F32 = jnp.float32
NZ = 8
NY = 4
BLK = 128
QUART = 256


def remote(src, dst, send, recv, device):
    return pltpu.make_async_remote_copy(
        src_ref=src, dst_ref=dst, send_sem=send, recv_sem=recv,
        device_id=device, device_id_type=MESH,
    )


def kernel(
    slot_of, feat_in, weight_in, cot_in, tiles_in,
    act_out, fgrad_out, wout_out,
    weight, cot, act, fgrad, wout, xg, hg, tiles, tiles_t, strip, part, acc, zq, zt,
    rr, rrx, rb, rbs, rbr, rc, rcs, rcr, rcx,
    vpart, vc, vcs, vcr, vcx, ws, wr, wxs, wxr, wfin,
    load_sem, feat_sem, store_sem,
    a_ys, a_yr, a_xs, a_xr, a_ds, a_dr,
    b_s, b_r, bx_s, bx_r, n_s, n_r, nx_s, nx_r,
    c_s, c_r, cx_s, cx_r,
    e_s, e_r, ex_s, ex_r, ed_s, ed_r,
    v_s, v_r, vx_s, vx_r, vd_s, vd_r,
    z_s, z_r, zx_s, zx_r, k_s, k_r, g_s, g_r, gd_s, gd_r,
):
    row = lax.axis_index("row")
    col = lax.axis_index("col")
    xl, z = row // NZ, row % NZ
    xh, y, core = col // 8, (col // 2) % NY, col % 2
    chip = xh * NY + y

    def z_dev(k):
        return (xl * NZ + (z + k + NZ) % NZ, col)

    def y_dev(d):
        return (row, xh * 8 + ((y + 1 - 2 * d + NY) % NY) * 2 + core)

    xl_dev = ((1 - xl) * NZ + z, col)
    xh_dev = (row, (1 - xh) * 8 + y * 2 + core)
    sib_dev = (row, xh * 8 + y * 2 + 1 - core)

    def chip_dev(k):
        other = (chip + k) % 8
        return (row, other * 2 + core)

    def feat_load(p, d):
        lanes = pl.ds((2 * p + d) * QUART, QUART)
        return pltpu.make_async_copy(
            feat_in.at[:, lanes], xg.at[p, d, pl.ds(pl.multiple_of(col * BLK, BLK), BLK)], feat_sem.at[p, d])

    loads = [
        pltpu.make_async_copy(tiles_in, tiles.at[pl.ds(0, 64)], load_sem.at[0]),
        pltpu.make_async_copy(weight_in, weight, load_sem.at[1]),
        pltpu.make_async_copy(cot_in, cot, load_sem.at[2]),
    ]
    barrier = pltpu.get_barrier_semaphore()
    peers = [chip_dev(k) for k in range(1, 8)] + [z_dev(k) for k in range(1, NZ)] + [xl_dev, sib_dev]
    for peer in peers:
        pl.semaphore_signal(barrier, inc=1, device_id=peer, device_id_type=MESH)
    for p in range(2):
        for d in range(2):
            feat_load(p, d).start()
    for load in loads:
        load.start()
    for p in range(2):
        for d in range(2):
            feat_load(p, d).wait()
    pl.semaphore_wait(barrier, len(peers))

    def col_source(d, sub, s, other):
        yy = (y + (2 * d - 1) * s + NY) % NY
        xx = xh if sub == 1 else 1 - xh
        return xx * 8 + yy * 2 + (1 - core if other else core)

    def xg_at(p, d, c):
        return xg.at[p, d, pl.ds(pl.multiple_of(c * BLK, BLK), BLK)]

    def ac_send(p, d, sub, s, to_y):
        here = xg_at(p, d, col_source(d, sub, s, False))
        if to_y:
            remote(here, here, a_ys.at[p, d, sub], a_yr.at[p, d, sub, s], y_dev(d)).start()
        else:
            remote(here, here, a_ds.at[p, d, sub], a_dr.at[p, d, sub, s], sib_dev).start()

    def ac_start(p):
        for d in range(2):
            ac_send(p, d, 1, 0, True)
            remote(xg_at(p, d, col), xg_at(p, d, col), a_xs.at[p, d], a_xr.at[p, d], xh_dev).start()
        for d in range(2):
            ac_send(p, d, 1, 0, False)

    def ac_event(p, e):
        sub, s = ((1, 1), (0, 0), (1, 2), (0, 1), (1, 3), (0, 2), (0, 3))[e]
        for d in range(2):
            here = xg_at(p, d, col_source(d, sub, s, False))
            if s == 0:
                remote(here, here, a_xs.at[p, d], a_xr.at[p, d], xh_dev).wait_recv()
            else:
                remote(here, here, a_ys.at[p, d, sub], a_yr.at[p, d, sub, s - 1], y_dev(d)).wait_recv()
            if s < NY - 1:
                ac_send(p, d, sub, s, True)
            ac_send(p, d, sub, s, False)

    def ac_finish(p):
        for sub in (1, 0):
            for s in range(NY):
                for d in range(2):
                    here = xg_at(p, d, col_source(d, sub, s, True))
                    remote(here, here, a_ds.at[p, d, sub], a_dr.at[p, d, sub, s], sib_dev).wait_recv()

    def product(source, table, first, step):
        for i in range(16):
            strip[:, i * BLK:(i + 1) * BLK] = table[slot_of[first + i * step]]
        return jnp.dot(strip[...], source, preferred_element_type=F32)

    def z_dest(d, s):
        return (z + (2 * d - 1) * (s + 1) + NZ) % NZ

    def row_step(s):
        def compute(q, inner):
            d, sub = q // 2, q % 2
            xd = xl + (1 - sub) * (1 - 2 * xl)
            part[0, q] = product(xg[0, d], tiles, (xd * NZ + z_dest(d, s)) * 16, 1)
            return inner

        def pass_on(q, inner):
            d, sub = q // 2, q % 2
            if s > 0:
                here = rr.at[q, s]
                remote(here, here, b_s.at[q], b_r.at[q, s - 1], z_dev(1 - 2 * d)).wait_recv()
                part[0, q] = part[0, q] + rr[q, s].astype(F32)
            rr[q, s] = part[0, q].astype(BF)
            if s < NZ - 1:
                remote(rr.at[q, s], rr.at[q, s + 1], b_s.at[q], b_r.at[q, s], z_dev(1 - 2 * d)).start()
            else:
                @pl.when(sub == 0)
                def _():
                    remote(rr.at[q, s], rrx.at[d], bx_s.at[d], bx_r.at[d], xl_dev).start()
            return inner

        lax.fori_loop(0, 4, compute, 0)
        lax.fori_loop(0, 4, pass_on, 0)

    def row_other(s):
        def one(d, inner):
            rbs[d, s] = product(xg[1, d], tiles, ((1 - xl) * NZ + z_dest(d, s)) * 16, 1).astype(BF)
            remote(rbs.at[d, s], rbr.at[d, s], nx_s.at[d], nx_r.at[d, s], xl_dev).start()
            return inner

        lax.fori_loop(0, 2, one, 0)

    def row_own(s):
        def one(d, inner):
            part[1, d] = product(xg[1, d], tiles, (xl * NZ + z_dest(d, s)) * 16, 1)
            return inner

        lax.fori_loop(0, 2, one, 0)

    def row_pass(s):
        def one(d, inner):
            here = rbr.at[d, s]
            remote(here, here, nx_s.at[d], nx_r.at[d, s], xl_dev).wait_recv()
            part[1, d] = part[1, d] + rbr[d, s].astype(F32)
            if s > 0:
                here = rb.at[d, s]
                remote(here, here, n_s.at[d], n_r.at[d, s - 1], z_dev(1 - 2 * d)).wait_recv()
                part[1, d] = part[1, d] + rb[d, s].astype(F32)
            if s < NZ - 1:
                rb[d, s] = part[1, d].astype(BF)
                remote(rb.at[d, s], rb.at[d, s + 1], n_s.at[d], n_r.at[d, s], z_dev(1 - 2 * d)).start()
            return inner

        lax.fori_loop(0, 2, one, 0)

    def row_finish(p):
        for d in range(2):
            if p == 0:
                remote(rrx.at[d], rrx.at[d], bx_s.at[d], bx_r.at[d], xl_dev).wait_recv()
                zq[d] = (part[0, 2 * d + 1] + rrx[d].astype(F32)).astype(BF)
            else:
                zq[2 + d] = part[1, d].astype(BF)
        both = jnp.concatenate([zq[2 * p], zq[2 * p + 1]], axis=1)
        value = jnp.dot(both, weight[pl.ds(p * 512, 512), :], preferred_element_type=F32)
        if p == 0:
            acc[...] = value
        else:
            acc[...] = acc[...] + value

    own_h = pl.ds(pl.multiple_of(row * BLK, BLK), BLK)

    def activate(p):
        for d in range(2):
            lanes = slice((2 * p + d) * QUART, (2 * p + d + 1) * QUART)
            hidden = acc[:, lanes]
            sig = 1.0 / (1.0 + jnp.exp(-hidden))
            act[:, lanes] = (hidden * sig).astype(BF)
            slope = sig * (1.0 + hidden * (1.0 - sig))
            hg[p, d, own_h, :] = (cot[:, lanes].astype(F32) * slope).astype(BF)

    def hg_at(p, d, sub, s):
        zz = (z + (2 * d - 1) * s + NZ) % NZ
        xx = xl if sub == 1 else 1 - xl
        return hg.at[p, d, pl.ds(pl.multiple_of((xx * NZ + zz) * BLK, BLK), BLK)]

    def ag_send(p, d, sub, s):
        here = hg_at(p, d, sub, s)
        remote(here, here, c_s.at[p, d, sub], c_r.at[p, d, sub, s], z_dev(1 - 2 * d)).start()

    def ag_cross(p, d, s):
        here = hg_at(p, d, 1, s)
        remote(here, here, cx_s.at[p, d], cx_r.at[p, d, s], xl_dev).start()

    def ag_start(p):
        for d in range(2):
            ag_send(p, d, 1, 0)
            ag_cross(p, d, 0)

    def ag_partner(p, s):
        for d in range(2):
            here = hg_at(p, d, 0, s)
            remote(here, here, cx_s.at[p, d], cx_r.at[p, d, s], xl_dev).wait_recv()
            if p == 0:
                ag_send(p, d, 0, 0)

    def ag_step(p, sub, s):
        for d in range(2):
            here = hg_at(p, d, sub, s)
            remote(here, here, c_s.at[p, d, sub], c_r.at[p, d, sub, s - 1], z_dev(1 - 2 * d)).wait_recv()
            if s < NZ - 1:
                ag_send(p, d, sub, s)
            if p == 1:
                ag_cross(p, d, s)

    def col_place(q, s):
        d, sub = q // 2, q % 2
        yd = (y + (2 * d - 1) * (s + 1) + NY) % NY
        xd = xh + (1 - sub) * (1 - 2 * xh)
        return d, sub, xd * NY + yd

    def col_compute(p, s):
        def other(q, inner):
            d, _, there = col_place(q, s)
            rcs[p, q, s] = product(hg[p, d], tiles_t, there * 2 + 1 - core, 16).astype(BF)
            remote(rcs.at[p, q, s], rcr.at[p, q, s], ed_s.at[p, q], ed_r.at[p, q, s], sib_dev).start()
            return inner

        def own(q, inner):
            d, _, there = col_place(q, s)
            part[p, q] = product(hg[p, d], tiles_t, there * 2 + core, 16)
            return inner

        lax.fori_loop(0, 4, other, 0)
        lax.fori_loop(0, 4, own, 0)

    def col_pass(p, s):
        def pass_on(q, inner):
            d, sub = q // 2, q % 2
            here = rcr.at[p, q, s]
            remote(here, here, ed_s.at[p, q], ed_r.at[p, q, s], sib_dev).wait_recv()
            part[p, q] = part[p, q] + rcr[p, q, s].astype(F32)
            if s > 0:
                here = rc.at[p, q, s]
                remote(here, here, e_s.at[p, q], e_r.at[p, q, s - 1], y_dev(d)).wait_recv()
                part[p, q] = part[p, q] + rc[p, q, s].astype(F32)
            rc[p, q, s] = part[p, q].astype(BF)
            if s < NY - 1:
                remote(rc.at[p, q, s], rc.at[p, q, s + 1], e_s.at[p, q], e_r.at[p, q, s], y_dev(d)).start()
            else:
                @pl.when(sub == 0)
                def _():
                    remote(rc.at[p, q, s], rcx.at[p, d], ex_s.at[p, d], ex_r.at[p, d], xh_dev).start()
            return inner

        lax.fori_loop(0, 4, pass_on, 0)

    def col_finish(p):
        delta = []
        for d in range(2):
            remote(rcx.at[p, d], rcx.at[p, d], ex_s.at[p, d], ex_r.at[p, d], xh_dev).wait_recv()
            delta.append((part[p, 2 * d + 1] + rcx[p, d].astype(F32)).astype(BF))
        value = lax.dot_general(
            jnp.concatenate(delta, axis=1), weight[:, pl.ds(p * 512, 512)],
            (((1,), (1,)), ((), ())), preferred_element_type=F32,
        )
        if p == 0:
            acc[...] = value
        else:
            fgrad[...] = (acc[...] + value).astype(BF)

    def turn_z():
        for k in range(8):
            zt[k] = zq[k // 2, :, (k % 2) * BLK:(k % 2 + 1) * BLK].T

    def wt_compute(s):
        def both(q, inner):
            d, _, there = col_place(q, s)
            tile = zt[there]
            vcs[q, s] = jnp.dot(tile, hg[1 - core, d, own_h, :], preferred_element_type=F32).astype(BF)
            remote(vcs.at[q, s], vcr.at[q, s], vd_s.at[q], vd_r.at[q, s], sib_dev).start()
            vpart[q] = jnp.dot(tile, hg[core, d, own_h, :], preferred_element_type=F32)
            return inner

        lax.fori_loop(0, 4, both, 0)

    def wt_pass(s):
        def pass_on(q, inner):
            d, sub = q // 2, q % 2
            here = vcr.at[q, s]
            remote(here, here, vd_s.at[q], vd_r.at[q, s], sib_dev).wait_recv()
            vpart[q] = vpart[q] + vcr[q, s].astype(F32)
            if s > 0:
                here = vc.at[q, s]
                remote(here, here, v_s.at[q], v_r.at[q, s - 1], y_dev(d)).wait_recv()
                vpart[q] = vpart[q] + vc[q, s].astype(F32)
            vc[q, s] = vpart[q].astype(BF)
            if s < NY - 1:
                remote(vc.at[q, s], vc.at[q, s + 1], v_s.at[q], v_r.at[q, s], y_dev(d)).start()
            else:
                @pl.when(sub == 0)
                def _():
                    remote(vc.at[q, s], vcx.at[d], vx_s.at[d], vx_r.at[d], xh_dev).start()
            return inner

        lax.fori_loop(0, 4, pass_on, 0)

    def wt_spread():
        for d in range(2):
            remote(vcx.at[d], vcx.at[d], vx_s.at[d], vx_r.at[d], xh_dev).wait_recv()
            value = (vpart[2 * d + 1] + vcx[d].astype(F32)).astype(BF)
            for k in range(NZ):
                ws[k, :, d * QUART:(d + 1) * QUART] = value[16 * k:16 * (k + 1), :]
        for k in range(1, NZ):
            remote(ws.at[(z + k) % NZ], wr.at[z], z_s, z_r.at[k], z_dev(k)).start()

    def wt_sum():
        total = ws[z].astype(F32)
        for k in range(1, NZ):
            zz = (z - k + NZ) % NZ
            remote(wr.at[zz], wr.at[zz], z_s, z_r.at[k], z_dev(k)).wait_recv()
            total = total + wr[zz].astype(F32)
        wxs[...] = total.astype(BF)
        remote(wxs, wxr, zx_s, zx_r, xl_dev).start()

    def wout_at(k, zz, side):
        lanes = pl.ds(pl.multiple_of(side * 512, 512), 512)
        return wout.at[k, zz, :, lanes]

    def wt_share():
        remote(wxr, wxr, zx_s, zx_r, xl_dev).wait_recv()
        value = (wxs[...].astype(F32) + wxr[...].astype(F32)).astype(BF)
        wfin[...] = value
        wout[chip, z, :, pl.ds(pl.multiple_of(core * 512, 512), 512)] = value
        for k in range(1, 8):
            remote(wfin, wout_at(chip, z, core), k_s, k_r.at[k], chip_dev(k)).start()

    def wz_at(k, side):
        lanes = pl.ds(pl.multiple_of(side * 512, 512), 512)
        return wout.at[:, (z + k + NZ) % NZ, :, lanes]

    def wz_send(d, s):
        here = wz_at((2 * d - 1) * s, core)
        if s < (NZ // 2 if d == 0 else NZ // 2 - 1):
            remote(here, here, g_s.at[d], g_r.at[d, s], z_dev(1 - 2 * d)).start()
        if s > 0 or d == 0:
            remote(here, here, gd_s, gd_r.at[d, s], sib_dev).start()

    def wz_start():
        for k in range(1, 8):
            there = wout_at((chip - k + 8) % 8, z, core)
            remote(there, there, k_s, k_r.at[k], chip_dev(k)).wait_recv()
        for d in range(2):
            wz_send(d, 0)

    def wz_step(s):
        for d in range(2):
            if s <= (NZ // 2 if d == 0 else NZ // 2 - 1):
                here = wz_at((2 * d - 1) * s, core)
                remote(here, here, g_s.at[d], g_r.at[d, s - 1], z_dev(1 - 2 * d)).wait_recv()
                wz_send(d, s)

    def wz_finish():
        for d in range(2):
            for s in range(NZ // 2 + 1 if d == 0 else NZ // 2):
                if s > 0 or d == 0:
                    here = wz_at((2 * d - 1) * s, 1 - core)
                    remote(here, here, gd_s, gd_r.at[d, s], sib_dev).wait_recv()

    def flip(lo, n):
        def one(t, carry):
            tiles_t[t] = tiles[t].T
            return carry
        lax.fori_loop(lo, lo + n, one, 0)

    ac_start(0)
    ac_start(1)
    loads[0].wait()
    tiles[64] = jnp.zeros((BLK, BLK), BF)
    tiles_t[64] = jnp.zeros((BLK, BLK), BF)
    ac_event(0, 0)
    for e in range(6):
        ac_event(0, e + 1)
        ac_event(1, e)
    ac_finish(0)
    row_step(0)
    ac_event(1, 6)
    ac_finish(1)
    loads[1].wait()
    loads[2].wait()
    row_other(0)
    row_own(0)
    for s in range(NZ):
        if s < NZ - 1:
            row_step(s + 1)
            row_other(s + 1)
        row_pass(s)
        if s < NZ - 1:
            row_own(s + 1)
        flip(8 * s, 8)
    row_finish(0)
    row_finish(1)
    activate(0)
    ag_start(0)
    activate(1)
    act_store = pltpu.make_async_copy(act, act_out, store_sem.at[0])
    act_store.start()
    ag_start(1)
    ag_partner(0, 0)
    turn_z()
    wt_compute(0)
    for s in range(1, NZ):
        ag_step(0, 1, s)
        ag_step(1, 1, s)
        ag_step(0, 0, s)
        if s == 2:
            wt_pass(0)
            wt_compute(1)
        if s == 3:
            wt_pass(1)
            wt_compute(2)
        if s == 5:
            wt_pass(2)
            wt_compute(3)
        if s == 6:
            wt_pass(3)
        if s == 7:
            wt_spread()
    col_compute(0, 0)
    for s in range(NZ):
        ag_partner(1, s)
    col_compute(1, 0)
    wt_sum()
    col_pass(0, 0)
    col_compute(0, 1)
    col_pass(1, 0)
    wt_share()
    col_compute(1, 1)
    col_pass(0, 1)
    col_compute(0, 2)
    wz_start()
    col_pass(1, 1)
    col_compute(1, 2)
    col_pass(0, 2)
    col_compute(0, 3)
    wz_step(1)
    col_pass(1, 2)
    col_compute(1, 3)
    wz_step(2)
    col_pass(0, 3)
    wz_step(3)
    col_pass(1, 3)
    col_finish(0)
    wz_step(4)
    col_finish(1)
    fgrad_store = pltpu.make_async_copy(fgrad, fgrad_out, store_sem.at[1])
    fgrad_store.start()
    wz_finish()
    wout_store = pltpu.make_async_copy(wout, wout_out, store_sem.at[2])
    wout_store.start()
    fgrad_store.wait()
    wout_store.wait()
    act_store.wait()

    for p in range(2):
        for d in range(2):
            for sub in range(2):
                q = 2 * d + sub
                sent = xg.at[p, d, pl.ds(0, 3 * BLK)]
                remote(sent, sent, a_ys.at[p, d, sub], a_yr.at[p, d, sub, 0], y_dev(d)).wait_send()
                sent = xg.at[p, d, pl.ds(0, 4 * BLK)]
                remote(sent, sent, a_ds.at[p, d, sub], a_dr.at[p, d, sub, 0], sib_dev).wait_send()
                if (p == 0 or sub == 1):
                    sent = hg.at[p, d, pl.ds(0, 7 * BLK)]
                    remote(sent, sent, c_s.at[p, d, sub], c_r.at[p, d, sub, 0], z_dev(1)).wait_send()
                sent = rc.at[p, q, pl.ds(0, NY - 1)]
                remote(sent, sent, e_s.at[p, q], e_r.at[p, q, 0], y_dev(d)).wait_send()
                remote(rcs.at[p, q], rcs.at[p, q], ed_s.at[p, q], ed_r.at[p, q, 0], sib_dev).wait_send()
            remote(xg_at(p, d, col), xg_at(p, d, col), a_xs.at[p, d], a_xr.at[p, d], xh_dev).wait_send()
            sent = hg.at[p, d, pl.ds(0, (8 if p else 1) * BLK)]
            remote(sent, sent, cx_s.at[p, d], cx_r.at[p, d, 0], xl_dev).wait_send()
            remote(rcx.at[p, d], rcx.at[p, d], ex_s.at[p, d], ex_r.at[p, d], xh_dev).wait_send()
    for q in range(4):
        sent = rr.at[q, pl.ds(0, NZ - 1)]
        remote(sent, sent, b_s.at[q], b_r.at[q, 0], z_dev(1)).wait_send()
    for d in range(2):
        sent = rb.at[d, pl.ds(0, NZ - 1)]
        remote(sent, sent, n_s.at[d], n_r.at[d, 0], z_dev(1)).wait_send()
        remote(rbs.at[d], rbs.at[d], nx_s.at[d], nx_r.at[d, 0], xl_dev).wait_send()
        remote(rrx.at[d], rrx.at[d], bx_s.at[d], bx_r.at[d], xl_dev).wait_send()
    for q in range(4):
        sent = vc.at[q, pl.ds(0, NY - 1)]
        remote(sent, sent, v_s.at[q], v_r.at[q, 0], y_dev(0)).wait_send()
        remote(vcs.at[q], vcs.at[q], vd_s.at[q], vd_r.at[q, 0], sib_dev).wait_send()
    for d in range(2):
        remote(vcx.at[d], vcx.at[d], vx_s.at[d], vx_r.at[d], xh_dev).wait_send()
    sent = wr.at[pl.ds(0, 7)]
    remote(sent, sent, z_s, z_r.at[1], z_dev(1)).wait_send()
    sent = wr.at[pl.ds(0, 7)]
    remote(sent, sent, k_s, k_r.at[1], chip_dev(1)).wait_send()
    remote(wxs, wxs, zx_s, zx_r, xl_dev).wait_send()
    for d in range(2):
        sent = wout.at[:, pl.ds(0, NZ // 2 - d), :, pl.ds(0, 512)]
        remote(sent, sent, g_s.at[d], g_r.at[d, 0], z_dev(1)).wait_send()
    sent = wout.at[:, :, :, pl.ds(0, 512)]
    remote(sent, sent, gd_s, gd_r.at[0, 0], sib_dev).wait_send()


def layer(slot_of, features, weight, cotangent, tiles):
    hbm = pl.BlockSpec(memory_space=pl.ANY)
    dma = pltpu.SemaphoreType.DMA
    chunk = (BLK, QUART)
    return pl.pallas_call(
        kernel,
        name="layer",
        out_shape=(
            jax.ShapeDtypeStruct((BLK, 1024), BF),
            jax.ShapeDtypeStruct((BLK, 1024), BF),
            jax.ShapeDtypeStruct((8, NZ, 16, 1024), BF),
        ),
        in_specs=[pl.BlockSpec(memory_space=pltpu.SMEM)] + [hbm] * 4,
        out_specs=(hbm, hbm, hbm),
        scratch_shapes=[
            pltpu.VMEM((1024, 1024), BF),
            pltpu.VMEM((BLK, 1024), BF),
            pltpu.VMEM((BLK, 1024), BF),
            pltpu.VMEM((BLK, 1024), BF),
            pltpu.VMEM((8, NZ, 16, 1024), BF),
            pltpu.VMEM((2, 2, 2048, QUART), BF),
            pltpu.VMEM((2, 2, 2048, QUART), BF),
            pltpu.VMEM((65, BLK, BLK), BF),
            pltpu.VMEM((65, BLK, BLK), BF),
            pltpu.VMEM((BLK, 2048), BF),
            pltpu.VMEM((2, 4, *chunk), F32),
            pltpu.VMEM((BLK, 1024), F32),
            pltpu.VMEM((4, *chunk), BF),
            pltpu.VMEM((8, BLK, BLK), BF),
            pltpu.VMEM((4, NZ, *chunk), BF),
            pltpu.VMEM((2, *chunk), BF),
            pltpu.VMEM((2, NZ, *chunk), BF),
            pltpu.VMEM((2, NZ, *chunk), BF),
            pltpu.VMEM((2, NZ, *chunk), BF),
            pltpu.VMEM((2, 4, NY, *chunk), BF),
            pltpu.VMEM((2, 4, NY, *chunk), BF),
            pltpu.VMEM((2, 4, NY, *chunk), BF),
            pltpu.VMEM((2, 2, *chunk), BF),
            pltpu.VMEM((4, *chunk), F32),
            pltpu.VMEM((4, NY, *chunk), BF),
            pltpu.VMEM((4, NY, *chunk), BF),
            pltpu.VMEM((4, NY, *chunk), BF),
            pltpu.VMEM((2, *chunk), BF),
            pltpu.VMEM((NZ, 16, 512), BF),
            pltpu.VMEM((NZ, 16, 512), BF),
            pltpu.VMEM((16, 512), BF),
            pltpu.VMEM((16, 512), BF),
            pltpu.VMEM((16, 512), BF),
            dma((3,)), dma((2, 2)), dma((3,)),
            dma((2, 2, 2)), dma((2, 2, 2, 3)), dma((2, 2)), dma((2, 2)), dma((2, 2, 2)), dma((2, 2, 2, 4)),
            dma((4,)), dma((4, 7)), dma((2,)), dma((2,)), dma((2,)), dma((2, 7)), dma((2,)), dma((2, 8)),
            dma((2, 2, 2)), dma((2, 2, 2, 7)), dma((2, 2)), dma((2, 2, 8)),
            dma((2, 4)), dma((2, 4, 3)), dma((2, 2)), dma((2, 2)), dma((2, 4)), dma((2, 4, 4)),
            dma((4,)), dma((4, 3)), dma((2,)), dma((2,)), dma((4,)), dma((4, 4)),
            dma, dma((NZ,)), dma, dma, dma, dma((NZ,)), dma((2,)), dma((2, 4)), dma, dma((2, 5)),
        ],
        compiler_params=pltpu.CompilerParams(
            collective_id=0, has_side_effects=True, vmem_limit_bytes=60 * 1024 * 1024,
        ),
    )(slot_of, features, weight, cotangent, tiles)


def on_device(features, weight, cotangent, tile_values, block_row, block_column, tile_count):
    slots = jnp.arange(64, dtype=jnp.int32)
    cell = block_row[0, 0] * 16 + block_column[0, 0]
    cell = jnp.where(slots < tile_count[0, 0], cell, -1)
    named = cell[None, :] == jnp.arange(256, dtype=jnp.int32)[:, None]
    slot_of = jnp.min(jnp.where(named, slots[None, :], 64), axis=1)
    activated, feat_grad, pieces = layer(slot_of, features, weight, cotangent, tile_values[0, 0])
    weight_grad = pieces.reshape(1024, 1024).astype(F32) * 32768 ** (-0.5)
    return activated, feat_grad, weight_grad


def solution(mesh):
    return jax.shard_map(
        on_device,
        mesh=mesh,
        in_specs=(
            P(("row", "col"), None),
            P(),
            P(("col", "row"), None),
            P("row", "col", None, None, None),
            P("row", "col", None),
            P("row", "col", None),
            P("row", "col"),
        ),
        out_specs=(P(("col", "row"), None), P(("row", "col"), None), P()),
        check_vma=False,
    )
```

```python
import jax
import jax.numpy as jnp
from jax import lax
from jax.experimental import pallas as pl
from jax.experimental.pallas import tpu as pltpu
from jax.sharding import PartitionSpec as P

MESH = pl.DeviceIdType.MESH
BF = jnp.bfloat16
F32 = jnp.float32
NZ = 8
NY = 4
BLK = 128
QUART = 256


def remote(src, dst, send, recv, device):
    return pltpu.make_async_remote_copy(
        src_ref=src, dst_ref=dst, send_sem=send, recv_sem=recv,
        device_id=device, device_id_type=MESH,
    )


def kernel(
    slot_of, feat_in, weight_in, cot_in, tiles_in,
    act_out, fgrad_out, wout_out,
    weight, cot, act, fgrad, wout, xg, hg, tiles, tiles_t, strip, acc, zq, zt,
    part, fin, rr, rrs, rrx, rb, rbs, rbr, rc, rcs, rcr, rcf, rcx,
    vpart, vfin, vc, vcs, vcr, vcf, vcx, ws, wr, wxs, wxr, wfin,
    load_sem, feat_sem, store_sem,
    a_ys, a_yr, a_xs, a_xr, a_ds, a_dr,
    b_s, b_r, bx_s, bx_r, n_s, n_r, nx_s, nx_r,
    c_s, c_r, cx_s, cx_r,
    e_s, e_r, ex_s, ex_r, ed_s, ed_r,
    v_s, v_r, vx_s, vx_r, vd_s, vd_r,
    z_s, z_r, zx_s, zx_r, k_s, k_r, g_s, g_r, gd_s, gd_r,
):
    row = lax.axis_index("row")
    col = lax.axis_index("col")
    xl, z = row // NZ, row % NZ
    xh, y, core = col // 8, (col // 2) % NY, col % 2
    chip = xh * NY + y

    def z_dev(k):
        return (xl * NZ + (z + k + NZ) % NZ, col)

    def y_dev(d):
        return (row, xh * 8 + ((y + 1 - 2 * d + NY) % NY) * 2 + core)

    xl_dev = ((1 - xl) * NZ + z, col)
    xh_dev = (row, (1 - xh) * 8 + y * 2 + core)
    sib_dev = (row, xh * 8 + y * 2 + 1 - core)

    def chip_dev(k):
        other = (chip + k) % 8
        return (row, other * 2 + core)

    def feat_load(p, d):
        lanes = pl.ds((2 * p + d) * QUART, QUART)
        return pltpu.make_async_copy(
            feat_in.at[:, lanes], xg.at[p, d, pl.ds(pl.multiple_of(col * BLK, BLK), BLK)], feat_sem.at[p, d])

    loads = [
        pltpu.make_async_copy(tiles_in, tiles.at[pl.ds(0, 64)], load_sem.at[0]),
        pltpu.make_async_copy(weight_in, weight, load_sem.at[1]),
        pltpu.make_async_copy(cot_in, cot, load_sem.at[2]),
    ]
    barrier = pltpu.get_barrier_semaphore()
    peers = [chip_dev(k) for k in range(1, 8)] + [z_dev(k) for k in range(1, NZ)] + [xl_dev, sib_dev]
    for peer in peers:
        pl.semaphore_signal(barrier, inc=1, device_id=peer, device_id_type=MESH)
    for p in range(2):
        for d in range(2):
            feat_load(p, d).start()
    for load in loads:
        load.start()
    for p in range(2):
        for d in range(2):
            feat_load(p, d).wait()
    pl.semaphore_wait(barrier, len(peers))

    def xg_at(p, h, sub, k, other):
        xx = xh if sub == 1 else 1 - xh
        c = xx * 8 + ((y + k + NY) % NY) * 2 + (1 - core if other else core)
        return xg.at[p, h, pl.ds(pl.multiple_of(c * BLK, BLK), BLK)]

    def ac_places(s):
        return [(e, h) for e in range(2) for h in ((e, 1 - e) if s == 1 else (e,))]

    def ac_sem(e, h, s):
        return 2 * e + h if s == 1 else 4 + e

    def ac_send(p, sub, e, h, s):
        here = xg_at(p, h, sub, (2 * e - 1) * s, False)
        remote(here, here, a_ys.at[p, sub, e], a_yr.at[p, sub, ac_sem(e, h, s + 1)], y_dev(e)).start()

    def ac_cross(p, sub, h, k, i):
        here = xg_at(p, h, sub, k, False)
        remote(here, here, a_ds.at[p, sub], a_dr.at[p, sub, i], sib_dev).start()

    def ac_first(p, sub):
        for e, h in ac_places(1):
            ac_send(p, sub, e, h, 0)

    def ac_start(p):
        ac_first(p, 1)
        for h in range(2):
            here = xg_at(p, h, 1, 0, False)
            remote(here, here, a_xs.at[p, h], a_xr.at[p, h], xh_dev).start()
        for h in range(2):
            ac_cross(p, 1, h, 0, h)

    def ac_event(p, i):
        sub, s = ((1, 1), (0, 0), (1, 2), (0, 1), (0, 2))[i]
        if s == 0:
            for h in range(2):
                here = xg_at(p, h, 0, 0, False)
                remote(here, here, a_xs.at[p, h], a_xr.at[p, h], xh_dev).wait_recv()
            ac_first(p, 0)
            for h in range(2):
                ac_cross(p, 0, h, 0, h)
            return
        for e, h in ac_places(s):
            k = (2 * e - 1) * s
            here = xg_at(p, h, sub, k, False)
            remote(here, here, a_ys.at[p, sub, e], a_yr.at[p, sub, ac_sem(e, h, s)], y_dev(e)).wait_recv()
            if s == 1 and h == e:
                ac_send(p, sub, e, h, 1)
            ac_cross(p, sub, h, k, 2 + ac_sem(e, h, s))

    def ac_finish(p):
        for sub in (1, 0):
            for h in range(2):
                here = xg_at(p, h, sub, 0, True)
                remote(here, here, a_ds.at[p, sub], a_dr.at[p, sub, h], sib_dev).wait_recv()
            for s in (1, 2):
                for e, h in ac_places(s):
                    here = xg_at(p, h, sub, (2 * e - 1) * s, True)
                    remote(here, here, a_ds.at[p, sub], a_dr.at[p, sub, 2 + ac_sem(e, h, s)], sib_dev).wait_recv()

    def lay(table, first, step):
        for i in range(16):
            strip[:, i * BLK:(i + 1) * BLK] = table[slot_of[first + i * step]]

    def times(source):
        return jnp.dot(strip[...], source, preferred_element_type=F32)

    class Ring:
        def __init__(self, reach, subs, term, ring_dev, terms, held, send, recv, cross=None):
            self.reach, self.subs, self.term, self.ring_dev = reach, subs, term, ring_dev
            self.terms, self.held, self.send, self.recv, self.cross = terms, held, send, recv, cross

        def split(self, q, s):
            e, sub = q // self.subs, q % self.subs
            return e, sub, (1 - 2 * e) * (self.reach - s), ((e,) if s == 0 else (e, 1 - e))

        def other(self, s):
            out, into, send, recv, dev = self.cross

            def one(q, inner):
                e, sub, k, hs = self.split(q, s)
                for h, value in zip(hs, self.term(False, e, sub, k, hs)):
                    out[q, h, s] = value.astype(BF)
                    remote(out.at[q, h, s], into.at[q, h, s], send.at[q], recv.at[q, h, s], dev).start()
                return inner

            lax.fori_loop(0, 2 * self.subs if s < self.reach else self.subs, one, 0)

        def own(self, s):
            def one(q, inner):
                e, sub, k, hs = self.split(q, s)
                for h, value in zip(hs, self.term(True, e, sub, k, hs)):
                    self.terms[q, h] = value
                return inner

            lax.fori_loop(0, 2 * self.subs, one, 0)

        def add_cross(self, q, h, s):
            if self.cross is None:
                return 0.0
            into, send, recv, dev = self.cross[1:]
            remote(into.at[q, h, s], into.at[q, h, s], send.at[q], recv.at[q, h, s], dev).wait_recv()
            return into[q, h, s].astype(F32)

        def add_ring(self, e, q, h, s):
            here = self.held.at[q, h, s]
            remote(here, here, self.send.at[q], self.recv.at[q, h, s - 1], self.ring_dev(e)).wait_recv()
            return self.held[q, h, s].astype(F32)

        def step(self, s):
            def one(q, inner):
                e, sub, k, hs = self.split(q, s)
                for i, h in enumerate(hs):
                    value = self.terms[q, h] + self.add_cross(q, h, s)
                    if s > i:
                        value = value + self.add_ring(e, q, h, s)
                    self.held[q, h, s] = value.astype(BF)
                    remote(self.held.at[q, h, s], self.held.at[q, h, s + 1], self.send.at[q],
                           self.recv.at[q, h, s], self.ring_dev(e)).start()
                return inner

            lax.fori_loop(0, 2 * self.subs, one, 0)

        def last_own(self, sums):
            def one(sub, inner):
                for h, value in zip((0, 1), self.term(True, 0, sub, 0, (0, 1))):
                    sums[sub, h] = value
                return inner

            lax.fori_loop(0, self.subs, one, 0)

        def last(self, sums, sub):
            for h in range(2):
                value = sums[sub, h] + self.add_cross(sub, h, self.reach)
                for e in range(2):
                    value = value + self.add_ring(e, e * self.subs + sub, h, self.reach)
                sums[sub, h] = value

        def drain(self):
            for q in range(2 * self.subs):
                sent = xg.at[0, 0, pl.ds(0, (2 * self.reach - 1) * BLK)]
                remote(sent, sent, self.send.at[q], self.recv.at[q, 0, 0], self.ring_dev(0)).wait_send()
                if self.cross is not None:
                    send, recv, dev = self.cross[2:]
                    count = 2 * self.reach - 1 + (2 if q < self.subs else 0)
                    sent = xg.at[0, 0, pl.ds(0, count * BLK)]
                    remote(sent, sent, send.at[q], recv.at[q, 0, 0], dev).wait_send()

    def z_ring_dev(e):
        return z_dev(1 - 2 * e)

    def row_term_0(mine, e, sub, k, hs):
        xd = xl + (1 - sub) * (1 - 2 * xl)
        lay(tiles, (xd * NZ + (z + k + NZ) % NZ) * 16, 1)
        return [times(xg[0, h]) for h in hs]

    row_a = Ring(NZ // 2, 2, row_term_0, z_ring_dev, part.at[0], rr, b_s, b_r)

    def row_term_1(mine, e, sub, k, hs):
        lay(tiles, ((xl if mine else 1 - xl) * NZ + (z + k + NZ) % NZ) * 16, 1)
        return [times(xg[1, h]) for h in hs]

    row_b = Ring(NZ // 2, 1, row_term_1, z_ring_dev, part.at[1], rb, n_s, n_r, (rbs, rbr, nx_s, nx_r, xl_dev))

    def row_send():
        row_a.last(fin.at[0], 0)
        for h in range(2):
            rrs[h] = fin[0, 0, h].astype(BF)
            remote(rrs.at[h], rrx.at[h], bx_s.at[h], bx_r.at[h], xl_dev).start()
        row_a.last(fin.at[0], 1)

    def row_finish(p):
        for h in range(2):
            if p == 0:
                remote(rrx.at[h], rrx.at[h], bx_s.at[h], bx_r.at[h], xl_dev).wait_recv()
                zq[h] = (fin[0, 1, h] + rrx[h].astype(F32)).astype(BF)
            else:
                zq[2 + h] = fin[1, 0, h].astype(BF)
        both = jnp.concatenate([zq[2 * p], zq[2 * p + 1]], axis=1)
        value = jnp.dot(both, weight[pl.ds(p * 512, 512), :], preferred_element_type=F32)
        if p == 0:
            acc[...] = value
        else:
            acc[...] = acc[...] + value

    own_h = pl.ds(pl.multiple_of(row * BLK, BLK), BLK)

    def activate(p):
        for d in range(2):
            lanes = slice((2 * p + d) * QUART, (2 * p + d + 1) * QUART)
            hidden = acc[:, lanes]
            sig = 1.0 / (1.0 + jnp.exp(-hidden))
            act[:, lanes] = (hidden * sig).astype(BF)
            slope = sig * (1.0 + hidden * (1.0 - sig))
            hg[p, d, own_h, :] = (cot[:, lanes].astype(F32) * slope).astype(BF)

    def hg_at(p, h, sub, k):
        xx = xl if sub == 1 else 1 - xl
        return hg.at[p, h, pl.ds(pl.multiple_of((xx * NZ + (z + k + NZ) % NZ) * BLK, BLK), BLK)]

    def ag_places(s):
        return [(e, h) for e in range(2) for h in (e, 1 - e) if s <= NZ // 2 - (h != e)]

    def ag_send(p, sub, e, h, s):
        here = hg_at(p, h, sub, (2 * e - 1) * s)
        remote(here, here, c_s.at[p, sub, e], c_r.at[p, sub, 2 * e + h, s], z_ring_dev(e)).start()

    def ag_cross(p, h, k, i):
        here = hg_at(p, h, 1, k)
        remote(here, here, cx_s.at[p], cx_r.at[p, i], xl_dev).start()

    def ag_cross_wait(p, h, k, i):
        here = hg_at(p, h, 0, k)
        remote(here, here, cx_s.at[p], cx_r.at[p, i], xl_dev).wait_recv()

    def ag_start(p):
        for e, h in ag_places(1):
            ag_send(p, 1, e, h, 0)
        for h in range(2):
            ag_cross(p, h, 0, h)

    def ag_partner(p):
        for h in range(2):
            ag_cross_wait(p, h, 0, h)
        if p == 0:
            for e, h in ag_places(1):
                ag_send(p, 0, e, h, 0)
        else:
            for s in range(1, NZ // 2 + 1):
                for e, h in ag_places(s):
                    ag_cross_wait(p, h, (2 * e - 1) * s, 4 * s + 2 * e + h - 2)

    def ag_step(p, sub, s):
        for e, h in ag_places(s):
            k = (2 * e - 1) * s
            here = hg_at(p, h, sub, k)
            remote(here, here, c_s.at[p, sub, e], c_r.at[p, sub, 2 * e + h, s - 1], z_ring_dev(e)).wait_recv()
            if (e, h) in ag_places(s + 1):
                ag_send(p, sub, e, h, s)
            if p == 1:
                ag_cross(p, h, k, 4 * s + 2 * e + h - 2)

    def col_place(sub, k):
        return (xh + (1 - sub) * (1 - 2 * xh)) * NY + (y + k + NY) % NY

    def col_ring(p):
        def term(mine, e, sub, k, hs):
            lay(tiles_t, col_place(sub, k) * 2 + (core if mine else 1 - core), 16)
            return [times(hg[p, h]) for h in hs]

        return Ring(NY // 2, 2, term, y_dev, part.at[p], rc.at[p], e_s.at[p], e_r.at[p],
                    (rcs.at[p], rcr.at[p], ed_s.at[p], ed_r.at[p], sib_dev))

    cols = [col_ring(0), col_ring(1)]

    def col_send(p):
        cols[p].last(fin.at[p], 0)
        for h in range(2):
            rcf[p, h] = fin[p, 0, h].astype(BF)
            remote(rcf.at[p, h], rcx.at[p, h], ex_s.at[p, h], ex_r.at[p, h], xh_dev).start()
        cols[p].last(fin.at[p], 1)

    def col_finish(p):
        delta = []
        for h in range(2):
            remote(rcx.at[p, h], rcx.at[p, h], ex_s.at[p, h], ex_r.at[p, h], xh_dev).wait_recv()
            delta.append((fin[p, 1, h] + rcx[p, h].astype(F32)).astype(BF))
        value = lax.dot_general(
            jnp.concatenate(delta, axis=1), weight[:, pl.ds(p * 512, 512)],
            (((1,), (1,)), ((), ())), preferred_element_type=F32,
        )
        if p == 0:
            acc[...] = value
        else:
            fgrad[...] = (acc[...] + value).astype(BF)

    def turn_z():
        for k in range(8):
            zt[k] = zq[k // 2, :, (k % 2) * BLK:(k % 2 + 1) * BLK].T

    def wt_term(mine, e, sub, k, hs):
        tile = zt[col_place(sub, k)]
        side = core if mine else 1 - core
        return [jnp.dot(tile, hg[side, h, own_h, :], preferred_element_type=F32) for h in hs]

    wts = Ring(NY // 2, 2, wt_term, y_dev, vpart, vc, v_s, v_r, (vcs, vcr, vd_s, vd_r, sib_dev))

    def wt_send():
        wts.last(vfin, 0)
        for h in range(2):
            vcf[h] = vfin[0, h].astype(BF)
            remote(vcf.at[h], vcx.at[h], vx_s.at[h], vx_r.at[h], xh_dev).start()
        wts.last(vfin, 1)

    def wt_spread():
        for d in range(2):
            remote(vcx.at[d], vcx.at[d], vx_s.at[d], vx_r.at[d], xh_dev).wait_recv()
            value = (vfin[1, d] + vcx[d].astype(F32)).astype(BF)
            for k in range(NZ):
                ws[k, :, d * QUART:(d + 1) * QUART] = value[16 * k:16 * (k + 1), :]
        for k in range(1, NZ):
            remote(ws.at[(z + k) % NZ], wr.at[z], z_s, z_r.at[k], z_dev(k)).start()

    def wt_sum():
        total = ws[z].astype(F32)
        for k in range(1, NZ):
            zz = (z - k + NZ) % NZ
            remote(wr.at[zz], wr.at[zz], z_s, z_r.at[k], z_dev(k)).wait_recv()
            total = total + wr[zz].astype(F32)
        wxs[...] = total.astype(BF)
        remote(wxs, wxr, zx_s, zx_r, xl_dev).start()

    def wout_at(k, zz, side):
        lanes = pl.ds(pl.multiple_of(side * 512, 512), 512)
        return wout.at[k, zz, :, lanes]

    def wt_share():
        remote(wxr, wxr, zx_s, zx_r, xl_dev).wait_recv()
        value = (wxs[...].astype(F32) + wxr[...].astype(F32)).astype(BF)
        wfin[...] = value
        wout[chip, z, :, pl.ds(pl.multiple_of(core * 512, 512), 512)] = value
        for k in range(1, 8):
            remote(wfin, wout_at(chip, z, core), k_s, k_r.at[k], chip_dev(k)).start()

    def wz_at(k, side):
        lanes = pl.ds(pl.multiple_of(side * 512, 512), 512)
        return wout.at[:, (z + k + NZ) % NZ, :, lanes]

    def wz_send(d, s):
        here = wz_at((2 * d - 1) * s, core)
        if s < (NZ // 2 if d == 0 else NZ // 2 - 1):
            remote(here, here, g_s.at[d], g_r.at[d, s], z_dev(1 - 2 * d)).start()
        if s > 0 or d == 0:
            remote(here, here, gd_s, gd_r.at[d, s], sib_dev).start()

    def wz_start():
        for k in range(1, 8):
            there = wout_at((chip - k + 8) % 8, z, core)
            remote(there, there, k_s, k_r.at[k], chip_dev(k)).wait_recv()
        for d in range(2):
            wz_send(d, 0)

    def wz_step(s):
        for d in range(2):
            if s <= (NZ // 2 if d == 0 else NZ // 2 - 1):
                here = wz_at((2 * d - 1) * s, core)
                remote(here, here, g_s.at[d], g_r.at[d, s - 1], z_dev(1 - 2 * d)).wait_recv()
                wz_send(d, s)

    def wz_finish():
        for d in range(2):
            for s in range(NZ // 2 + 1 if d == 0 else NZ // 2):
                if s > 0 or d == 0:
                    here = wz_at((2 * d - 1) * s, 1 - core)
                    remote(here, here, gd_s, gd_r.at[d, s], sib_dev).wait_recv()

    def flip(lo, n):
        def one(t, carry):
            tiles_t[t] = tiles[t].T
            return carry
        lax.fori_loop(lo, lo + n, one, 0)

    ac_start(0)
    ac_start(1)
    loads[0].wait()
    tiles[64] = jnp.zeros((BLK, BLK), BF)
    tiles_t[64] = jnp.zeros((BLK, BLK), BF)
    ac_event(0, 0)
    ac_event(0, 1)
    ac_event(1, 0)
    ac_event(0, 2)
    ac_event(1, 1)
    ac_event(0, 3)
    ac_event(1, 2)
    ac_event(0, 4)
    ac_event(1, 3)
    ac_finish(0)
    row_a.own(0)
    row_a.step(0)
    ac_event(1, 4)
    ac_finish(1)
    loads[1].wait()
    loads[2].wait()
    row_b.other(0)
    row_a.own(1)
    row_b.other(1)
    row_b.own(0)
    row_a.step(1)
    row_b.step(0)
    flip(0, 20)
    for s in range(1, NZ // 2):
        if s < NZ // 2 - 1:
            row_a.own(s + 1)
            row_b.other(s + 1)
        else:
            row_a.last_own(fin.at[0])
            row_b.other(s + 1)
        row_b.own(s)
        if s < NZ // 2 - 1:
            row_a.step(s + 1)
        else:
            row_send()
        row_b.step(s)
        if s < NZ // 2 - 1:
            flip(20 * s, 20)
    row_b.last_own(fin.at[1])
    flip(60, 4)
    row_finish(0)
    row_b.last(fin.at[1], 0)
    row_finish(1)
    activate(0)
    ag_start(0)
    activate(1)
    act_store = pltpu.make_async_copy(act, act_out, store_sem.at[0])
    act_store.start()
    ag_start(1)
    ag_partner(0)
    turn_z()
    wts.other(0)
    wts.own(0)
    for s in range(1, NZ // 2 + 1):
        ag_step(0, 1, s)
        if s == 1:
            wts.step(0)
            wts.other(1)
            wts.own(1)
        if s == 2:
            wt_send()
        ag_step(1, 1, s)
        if s == 1:
            wts.step(1)
            wts.other(2)
            wts.last_own(vfin)
        if s == 2:
            wt_spread()
        ag_step(0, 0, s)
        if s == 3:
            wt_sum()
    wt_share()
    cols[0].other(0)
    cols[0].own(0)
    wz_start()
    ag_partner(1)
    cols[1].other(0)
    cols[1].own(0)
    cols[0].step(0)
    cols[0].other(1)
    cols[0].own(1)
    cols[1].step(0)
    wz_step(1)
    cols[1].other(1)
    cols[1].own(1)
    cols[0].step(1)
    cols[0].other(2)
    cols[0].last_own(fin.at[0])
    cols[1].step(1)
    wz_step(2)
    cols[1].other(2)
    cols[1].last_own(fin.at[1])
    col_send(0)
    wz_step(3)
    col_send(1)
    col_finish(0)
    wz_step(4)
    col_finish(1)
    fgrad_store = pltpu.make_async_copy(fgrad, fgrad_out, store_sem.at[1])
    fgrad_store.start()
    wz_finish()
    wout_store = pltpu.make_async_copy(wout, wout_out, store_sem.at[2])
    wout_store.start()
    fgrad_store.wait()
    wout_store.wait()
    act_store.wait()

    for p in range(2):
        for sub in range(2):
            for e in range(2):
                sent = xg.at[0, 0, pl.ds(0, 3 * BLK)]
                remote(sent, sent, a_ys.at[p, sub, e], a_yr.at[p, sub, 0], y_dev(e)).wait_send()
                if (p == 0 or sub == 1):
                    sent = hg.at[0, 0, pl.ds(0, 7 * BLK)]
                    remote(sent, sent, c_s.at[p, sub, e], c_r.at[p, sub, 0, 0], z_dev(1)).wait_send()
            sent = xg.at[0, 0, pl.ds(0, 8 * BLK)]
            remote(sent, sent, a_ds.at[p, sub], a_dr.at[p, sub, 0], sib_dev).wait_send()
        for h in range(2):
            sent = xg.at[0, 0, pl.ds(0, BLK)]
            remote(sent, sent, a_xs.at[p, h], a_xr.at[p, h], xh_dev).wait_send()
            remote(rcx.at[p, h], rcx.at[p, h], ex_s.at[p, h], ex_r.at[p, h], xh_dev).wait_send()
        sent = hg.at[0, 0, pl.ds(0, (16 if p else 2) * BLK)]
        remote(sent, sent, cx_s.at[p], cx_r.at[p, 0], xl_dev).wait_send()
        cols[p].drain()
    row_a.drain()
    row_b.drain()
    for h in range(2):
        remote(rrx.at[h], rrx.at[h], bx_s.at[h], bx_r.at[h], xl_dev).wait_send()
    wts.drain()
    for h in range(2):
        remote(vcx.at[h], vcx.at[h], vx_s.at[h], vx_r.at[h], xh_dev).wait_send()
    sent = wr.at[pl.ds(0, 7)]
    remote(sent, sent, z_s, z_r.at[1], z_dev(1)).wait_send()
    sent = wr.at[pl.ds(0, 7)]
    remote(sent, sent, k_s, k_r.at[1], chip_dev(1)).wait_send()
    remote(wxs, wxs, zx_s, zx_r, xl_dev).wait_send()
    for d in range(2):
        sent = wout.at[:, pl.ds(0, NZ // 2 - d), :, pl.ds(0, 512)]
        remote(sent, sent, g_s.at[d], g_r.at[d, 0], z_dev(1)).wait_send()
    sent = wout.at[:, :, :, pl.ds(0, 512)]
    remote(sent, sent, gd_s, gd_r.at[0, 0], sib_dev).wait_send()


def layer(slot_of, features, weight, cotangent, tiles):
    hbm = pl.BlockSpec(memory_space=pl.ANY)
    dma = pltpu.SemaphoreType.DMA
    chunk = (BLK, QUART)
    return pl.pallas_call(
        kernel,
        name="layer",
        out_shape=(
            jax.ShapeDtypeStruct((BLK, 1024), BF),
            jax.ShapeDtypeStruct((BLK, 1024), BF),
            jax.ShapeDtypeStruct((8, NZ, 16, 1024), BF),
        ),
        in_specs=[pl.BlockSpec(memory_space=pltpu.SMEM)] + [hbm] * 4,
        out_specs=(hbm, hbm, hbm),
        scratch_shapes=[
            pltpu.VMEM((1024, 1024), BF),
            pltpu.VMEM((BLK, 1024), BF),
            pltpu.VMEM((BLK, 1024), BF),
            pltpu.VMEM((BLK, 1024), BF),
            pltpu.VMEM((8, NZ, 16, 1024), BF),
            pltpu.VMEM((2, 2, 2048, QUART), BF),
            pltpu.VMEM((2, 2, 2048, QUART), BF),
            pltpu.VMEM((65, BLK, BLK), BF),
            pltpu.VMEM((65, BLK, BLK), BF),
            pltpu.VMEM((BLK, 2048), BF),
            pltpu.VMEM((BLK, 1024), F32),
            pltpu.VMEM((4, *chunk), BF),
            pltpu.VMEM((8, BLK, BLK), BF),
            pltpu.VMEM((2, 4, 2, *chunk), F32),
            pltpu.VMEM((2, 2, 2, *chunk), F32),
            pltpu.VMEM((4, 2, 5, *chunk), BF),
            pltpu.VMEM((2, *chunk), BF),
            pltpu.VMEM((2, *chunk), BF),
            pltpu.VMEM((2, 2, 5, *chunk), BF),
            pltpu.VMEM((2, 2, 5, *chunk), BF),
            pltpu.VMEM((2, 2, 5, *chunk), BF),
            pltpu.VMEM((2, 4, 2, 3, *chunk), BF),
            pltpu.VMEM((2, 4, 2, 3, *chunk), BF),
            pltpu.VMEM((2, 4, 2, 3, *chunk), BF),
            pltpu.VMEM((2, 2, *chunk), BF),
            pltpu.VMEM((2, 2, *chunk), BF),
            pltpu.VMEM((4, 2, *chunk), F32),
            pltpu.VMEM((2, 2, *chunk), F32),
            pltpu.VMEM((4, 2, 3, *chunk), BF),
            pltpu.VMEM((4, 2, 3, *chunk), BF),
            pltpu.VMEM((4, 2, 3, *chunk), BF),
            pltpu.VMEM((2, *chunk), BF),
            pltpu.VMEM((2, *chunk), BF),
            pltpu.VMEM((NZ, 16, 512), BF),
            pltpu.VMEM((NZ, 16, 512), BF),
            pltpu.VMEM((16, 512), BF),
            pltpu.VMEM((16, 512), BF),
            pltpu.VMEM((16, 512), BF),
            dma((3,)), dma((2, 2)), dma((3,)),
            dma((2, 2, 2)), dma((2, 2, 6)), dma((2, 2)), dma((2, 2)), dma((2, 2)), dma((2, 2, 8)),
            dma((4,)), dma((4, 2, 4)), dma((2,)), dma((2,)), dma((2,)), dma((2, 2, 4)), dma((2,)), dma((2, 2, 5)),
            dma((2, 2, 2)), dma((2, 2, 4, 4)), dma((2,)), dma((2, 18)),
            dma((2, 4)), dma((2, 4, 2, 2)), dma((2, 2)), dma((2, 2)), dma((2, 4)), dma((2, 4, 2, 3)),
            dma((4,)), dma((4, 2, 2)), dma((2,)), dma((2,)), dma((4,)), dma((4, 2, 3)),
            dma, dma((NZ,)), dma, dma, dma, dma((NZ,)), dma((2,)), dma((2, 4)), dma, dma((2, 5)),
        ],
        compiler_params=pltpu.CompilerParams(
            collective_id=0, has_side_effects=True, vmem_limit_bytes=60 * 1024 * 1024,
        ),
    )(slot_of, features, weight, cotangent, tiles)


def on_device(features, weight, cotangent, tile_values, block_row, block_column, tile_count):
    slots = jnp.arange(64, dtype=jnp.int32)
    cell = block_row[0, 0] * 16 + block_column[0, 0]
    cell = jnp.where(slots < tile_count[0, 0], cell, -1)
    named = cell[None, :] == jnp.arange(256, dtype=jnp.int32)[:, None]
    slot_of = jnp.min(jnp.where(named, slots[None, :], 64), axis=1)
    activated, feat_grad, pieces = layer(slot_of, features, weight, cotangent, tile_values[0, 0])
    weight_grad = pieces.reshape(1024, 1024).astype(F32) * 32768 ** (-0.5)
    return activated, feat_grad, weight_grad


def solution(mesh):
    return jax.shard_map(
        on_device,
        mesh=mesh,
        in_specs=(
            P(("row", "col"), None),
            P(),
            P(("col", "row"), None),
            P("row", "col", None, None, None),
            P("row", "col", None),
            P("row", "col", None),
            P("row", "col"),
        ),
        out_specs=(P(("col", "row"), None), P(("row", "col"), None), P()),
        check_vma=False,
    )
```

```python
import jax
import jax.numpy as jnp
from jax import lax
from jax.experimental import pallas as pl
from jax.experimental.pallas import tpu as pltpu
from jax.sharding import PartitionSpec as P

MESH = pl.DeviceIdType.MESH
BF = jnp.bfloat16
F32 = jnp.float32
NZ = 8
NY = 4
BLK = 128
QUART = 256


def remote(src, dst, send, recv, device):
    return pltpu.make_async_remote_copy(
        src_ref=src, dst_ref=dst, send_sem=send, recv_sem=recv,
        device_id=device, device_id_type=MESH,
    )


def kernel(
    slot_of, feat_in, weight_in, cot_in, tiles_in,
    act_out, fgrad_out, wout_out,
    weight, cot, act, fgrad, wout, xg, hg, tiles, tiles_t, strip, acc, zq, zt,
    part, fin, rr, rrs, rrx, rb, rbs, rbr, rc, rcs, rcr, rcf, rcx,
    vpart, vfin, vc, vcs, vcr, vcf, vcx, ws, wr, wxs, wxr, wfin,
    load_sem, feat_sem, store_sem,
    a_ys, a_yr, a_xs, a_xr, a_ds, a_dr,
    b_s, b_r, bx_s, bx_r, n_s, n_r, nx_s, nx_r,
    c_s, c_r, cx_s, cx_r,
    e_s, e_r, ex_s, ex_r, ed_s, ed_r,
    v_s, v_r, vx_s, vx_r, vd_s, vd_r,
    z_s, z_r, zx_s, zx_r, k_s, k_r, g_s, g_r, gd_s, gd_r,
):
    row = lax.axis_index("row")
    col = lax.axis_index("col")
    xl, z = row // NZ, row % NZ
    xh, y, core = col // 8, (col // 2) % NY, col % 2
    chip = xh * NY + y

    def z_dev(k):
        return (xl * NZ + (z + k + NZ) % NZ, col)

    def y_dev(d):
        return (row, xh * 8 + ((y + 1 - 2 * d + NY) % NY) * 2 + core)

    xl_dev = ((1 - xl) * NZ + z, col)
    xh_dev = (row, (1 - xh) * 8 + y * 2 + core)
    sib_dev = (row, xh * 8 + y * 2 + 1 - core)

    def chip_dev(k):
        other = (chip + k) % 8
        return (row, other * 2 + core)

    def feat_load(p, d):
        lanes = pl.ds((2 * p + d) * QUART, QUART)
        return pltpu.make_async_copy(
            feat_in.at[:, lanes], xg.at[p, d, pl.ds(pl.multiple_of(col * BLK, BLK), BLK)], feat_sem.at[p, d])

    loads = [
        pltpu.make_async_copy(tiles_in, tiles.at[pl.ds(0, 64)], load_sem.at[0]),
        pltpu.make_async_copy(weight_in, weight, load_sem.at[1]),
        pltpu.make_async_copy(cot_in, cot, load_sem.at[2]),
    ]
    barrier = pltpu.get_barrier_semaphore()
    peers = [chip_dev(k) for k in range(1, 8)] + [z_dev(k) for k in range(1, NZ)] + [xl_dev, sib_dev]
    for peer in peers:
        pl.semaphore_signal(barrier, inc=1, device_id=peer, device_id_type=MESH)
    for p in range(2):
        for d in range(2):
            feat_load(p, d).start()
    for load in loads:
        load.start()
    for p in range(2):
        for d in range(2):
            feat_load(p, d).wait()
    pl.semaphore_wait(barrier, len(peers))

    def xg_at(p, h, sub, k, other):
        xx = xh if sub == 1 else 1 - xh
        c = xx * 8 + ((y + k + NY) % NY) * 2 + (1 - core if other else core)
        return xg.at[p, h, pl.ds(pl.multiple_of(c * BLK, BLK), BLK)]

    def ac_places(s):
        return [(e, h) for e in range(2) for h in ((e, 1 - e) if s == 1 else (e,))]

    def ac_sem(e, h, s):
        return 2 * e + h if s == 1 else 4 + e

    def ac_send(p, sub, e, h, s):
        here = xg_at(p, h, sub, (2 * e - 1) * s, False)
        remote(here, here, a_ys.at[p, sub, e], a_yr.at[p, sub, ac_sem(e, h, s + 1)], y_dev(e)).start()

    def ac_cross(p, sub, h, k, i):
        here = xg_at(p, h, sub, k, False)
        remote(here, here, a_ds.at[p, sub], a_dr.at[p, sub, i], sib_dev).start()

    def ac_first(p, sub):
        for e, h in ac_places(1):
            ac_send(p, sub, e, h, 0)

    def ac_start(p):
        ac_first(p, 1)
        for h in range(2):
            ac_over(p, h, 0, h)
        for h in range(2):
            ac_cross(p, 1, h, 0, h)

    def ac_over(p, h, k, i):
        here = xg_at(p, h, 1, k, False)
        remote(here, here, a_xs.at[p], a_xr.at[p, i], xh_dev).start()

    def ac_over_wait(p, h, k, i):
        here = xg_at(p, h, 0, k, False)
        remote(here, here, a_xs.at[p], a_xr.at[p, i], xh_dev).wait_recv()

    def ac_event(p, i):
        sub, s = ((1, 1), (0, 0), (1, 2), (0, 1), (0, 2))[i]
        if s == 0:
            for h in range(2):
                ac_over_wait(p, h, 0, h)
            if p == 0:
                ac_first(p, 0)
            for h in range(2):
                ac_cross(p, 0, h, 0, h)
            return
        for e, h in ac_places(s):
            k = (2 * e - 1) * s
            i = 2 + ac_sem(e, h, s)
            if p == 1 and sub == 0:
                ac_over_wait(p, h, k, i)
            else:
                here = xg_at(p, h, sub, k, False)
                remote(here, here, a_ys.at[p, sub, e], a_yr.at[p, sub, i - 2], y_dev(e)).wait_recv()
                if s == 1 and h == e:
                    ac_send(p, sub, e, h, 1)
                if p == 1:
                    ac_over(p, h, k, i)
            ac_cross(p, sub, h, k, i)

    def ac_finish(p):
        for sub in (1, 0):
            for h in range(2):
                here = xg_at(p, h, sub, 0, True)
                remote(here, here, a_ds.at[p, sub], a_dr.at[p, sub, h], sib_dev).wait_recv()
            for s in (1, 2):
                for e, h in ac_places(s):
                    here = xg_at(p, h, sub, (2 * e - 1) * s, True)
                    remote(here, here, a_ds.at[p, sub], a_dr.at[p, sub, 2 + ac_sem(e, h, s)], sib_dev).wait_recv()

    def lay(table, first, step):
        for i in range(16):
            strip[:, i * BLK:(i + 1) * BLK] = table[slot_of[first + i * step]]

    def times(source):
        return jnp.dot(strip[...], source, preferred_element_type=F32)

    class Ring:
        def __init__(self, reach, subs, term, ring_dev, terms, held, send, recv, cross=None):
            self.reach, self.subs, self.term, self.ring_dev = reach, subs, term, ring_dev
            self.terms, self.held, self.send, self.recv, self.cross = terms, held, send, recv, cross

        def split(self, q, s):
            e, sub = q // self.subs, q % self.subs
            return e, sub, (1 - 2 * e) * (self.reach - s), ((e,) if s == 0 else (e, 1 - e))

        def other(self, s):
            out, into, send, recv, dev = self.cross

            def one(q, inner):
                e, sub, k, hs = self.split(q, s)
                for h, value in zip(hs, self.term(False, e, sub, k, hs)):
                    out[q, h, s] = value.astype(BF)
                    remote(out.at[q, h, s], into.at[q, h, s], send.at[q], recv.at[q, h, s], dev).start()
                return inner

            lax.fori_loop(0, 2 * self.subs if s < self.reach else self.subs, one, 0)

        def own(self, s):
            def one(q, inner):
                e, sub, k, hs = self.split(q, s)
                for h, value in zip(hs, self.term(True, e, sub, k, hs)):
                    self.terms[q, h] = value
                return inner

            lax.fori_loop(0, 2 * self.subs, one, 0)

        def add_cross(self, q, h, s):
            if self.cross is None:
                return 0.0
            into, send, recv, dev = self.cross[1:]
            remote(into.at[q, h, s], into.at[q, h, s], send.at[q], recv.at[q, h, s], dev).wait_recv()
            return into[q, h, s].astype(F32)

        def add_ring(self, e, q, h, s):
            here = self.held.at[q, h, s]
            remote(here, here, self.send.at[q], self.recv.at[q, h, s - 1], self.ring_dev(e)).wait_recv()
            return self.held[q, h, s].astype(F32)

        def step(self, s):
            def one(q, inner):
                e, sub, k, hs = self.split(q, s)
                for i, h in enumerate(hs):
                    value = self.terms[q, h] + self.add_cross(q, h, s)
                    if s > i:
                        value = value + self.add_ring(e, q, h, s)
                    self.held[q, h, s] = value.astype(BF)
                    remote(self.held.at[q, h, s], self.held.at[q, h, s + 1], self.send.at[q],
                           self.recv.at[q, h, s], self.ring_dev(e)).start()
                return inner

            lax.fori_loop(0, 2 * self.subs, one, 0)

        def last_own(self, sums):
            def one(sub, inner):
                for h, value in zip((0, 1), self.term(True, 0, sub, 0, (0, 1))):
                    sums[sub, h] = value
                return inner

            lax.fori_loop(0, self.subs, one, 0)

        def last(self, sums, sub):
            for h in range(2):
                value = sums[sub, h] + self.add_cross(sub, h, self.reach)
                for e in range(2):
                    value = value + self.add_ring(e, e * self.subs + sub, h, self.reach)
                sums[sub, h] = value

        def drain(self):
            for q in range(2 * self.subs):
                sent = xg.at[0, 0, pl.ds(0, (2 * self.reach - 1) * BLK)]
                remote(sent, sent, self.send.at[q], self.recv.at[q, 0, 0], self.ring_dev(0)).wait_send()
                if self.cross is not None:
                    send, recv, dev = self.cross[2:]
                    count = 2 * self.reach - 1 + (2 if q < self.subs else 0)
                    sent = xg.at[0, 0, pl.ds(0, count * BLK)]
                    remote(sent, sent, send.at[q], recv.at[q, 0, 0], dev).wait_send()

    def z_ring_dev(e):
        return z_dev(1 - 2 * e)

    def row_term_0(mine, e, sub, k, hs):
        xd = xl + (1 - sub) * (1 - 2 * xl)
        lay(tiles, (xd * NZ + (z + k + NZ) % NZ) * 16, 1)
        return [times(xg[0, h]) for h in hs]

    row_a = Ring(NZ // 2, 2, row_term_0, z_ring_dev, part.at[0], rr, b_s, b_r)

    def row_term_1(mine, e, sub, k, hs):
        lay(tiles, ((xl if mine else 1 - xl) * NZ + (z + k + NZ) % NZ) * 16, 1)
        return [times(xg[1, h]) for h in hs]

    row_b = Ring(NZ // 2, 1, row_term_1, z_ring_dev, part.at[1], rb, n_s, n_r, (rbs, rbr, nx_s, nx_r, xl_dev))

    def row_send():
        row_a.last(fin.at[0], 0)
        for h in range(2):
            rrs[h] = fin[0, 0, h].astype(BF)
            remote(rrs.at[h], rrx.at[h], bx_s.at[h], bx_r.at[h], xl_dev).start()
        row_a.last(fin.at[0], 1)

    def row_finish(p):
        for h in range(2):
            if p == 0:
                remote(rrx.at[h], rrx.at[h], bx_s.at[h], bx_r.at[h], xl_dev).wait_recv()
                zq[h] = (fin[0, 1, h] + rrx[h].astype(F32)).astype(BF)
            else:
                zq[2 + h] = fin[1, 0, h].astype(BF)
        both = jnp.concatenate([zq[2 * p], zq[2 * p + 1]], axis=1)
        value = jnp.dot(both, weight[pl.ds(p * 512, 512), :], preferred_element_type=F32)
        if p == 0:
            acc[...] = value
        else:
            acc[...] = acc[...] + value

    own_h = pl.ds(pl.multiple_of(row * BLK, BLK), BLK)

    def activate(p):
        for d in range(2):
            lanes = slice((2 * p + d) * QUART, (2 * p + d + 1) * QUART)
            hidden = acc[:, lanes]
            sig = 1.0 / (1.0 + jnp.exp(-hidden))
            act[:, lanes] = (hidden * sig).astype(BF)
            slope = sig * (1.0 + hidden * (1.0 - sig))
            hg[p, d, own_h, :] = (cot[:, lanes].astype(F32) * slope).astype(BF)

    def hg_at(p, h, sub, k):
        xx = xl if sub == 1 else 1 - xl
        return hg.at[p, h, pl.ds(pl.multiple_of((xx * NZ + (z + k + NZ) % NZ) * BLK, BLK), BLK)]

    def ag_places(s):
        return [(e, h) for e in range(2) for h in (e, 1 - e) if s <= NZ // 2 - (h != e)]

    def ag_send(p, sub, e, h, s):
        here = hg_at(p, h, sub, (2 * e - 1) * s)
        remote(here, here, c_s.at[p, sub, e], c_r.at[p, sub, 2 * e + h, s], z_ring_dev(e)).start()

    def ag_cross(p, h, k, i):
        here = hg_at(p, h, 1, k)
        remote(here, here, cx_s.at[p], cx_r.at[p, i], xl_dev).start()

    def ag_cross_wait(p, h, k, i):
        here = hg_at(p, h, 0, k)
        remote(here, here, cx_s.at[p], cx_r.at[p, i], xl_dev).wait_recv()

    def ag_start(p):
        for e, h in ag_places(1):
            ag_send(p, 1, e, h, 0)
        for h in range(2):
            ag_cross(p, h, 0, h)

    def ag_partner(p):
        for h in range(2):
            ag_cross_wait(p, h, 0, h)
        if p == 0:
            for e, h in ag_places(1):
                ag_send(p, 0, e, h, 0)
        else:
            for s in range(1, NZ // 2 + 1):
                for e, h in ag_places(s):
                    ag_cross_wait(p, h, (2 * e - 1) * s, 4 * s + 2 * e + h - 2)

    def ag_step(p, sub, s):
        for e, h in ag_places(s):
            k = (2 * e - 1) * s
            here = hg_at(p, h, sub, k)
            remote(here, here, c_s.at[p, sub, e], c_r.at[p, sub, 2 * e + h, s - 1], z_ring_dev(e)).wait_recv()
            if (e, h) in ag_places(s + 1):
                ag_send(p, sub, e, h, s)
            if p == 1:
                ag_cross(p, h, k, 4 * s + 2 * e + h - 2)

    def col_place(sub, k):
        return (xh + (1 - sub) * (1 - 2 * xh)) * NY + (y + k + NY) % NY

    def col_ring(p):
        def term(mine, e, sub, k, hs):
            lay(tiles_t, col_place(sub, k) * 2 + (core if mine else 1 - core), 16)
            return [times(hg[p, h]) for h in hs]

        return Ring(NY // 2, 2, term, y_dev, part.at[p], rc.at[p], e_s.at[p], e_r.at[p],
                    (rcs.at[p], rcr.at[p], ed_s.at[p], ed_r.at[p], sib_dev))

    cols = [col_ring(0), col_ring(1)]

    def col_send(p):
        cols[p].last(fin.at[p], 0)
        for h in range(2):
            rcf[p, h] = fin[p, 0, h].astype(BF)
            remote(rcf.at[p, h], rcx.at[p, h], ex_s.at[p, h], ex_r.at[p, h], xh_dev).start()
        cols[p].last(fin.at[p], 1)

    def col_finish(p):
        delta = []
        for h in range(2):
            remote(rcx.at[p, h], rcx.at[p, h], ex_s.at[p, h], ex_r.at[p, h], xh_dev).wait_recv()
            delta.append((fin[p, 1, h] + rcx[p, h].astype(F32)).astype(BF))
        value = lax.dot_general(
            jnp.concatenate(delta, axis=1), weight[:, pl.ds(p * 512, 512)],
            (((1,), (1,)), ((), ())), preferred_element_type=F32,
        )
        if p == 0:
            acc[...] = value
        else:
            fgrad[...] = (acc[...] + value).astype(BF)

    def turn_z():
        for k in range(8):
            zt[k] = zq[k // 2, :, (k % 2) * BLK:(k % 2 + 1) * BLK].T

    def wt_term(mine, e, sub, k, hs):
        tile = zt[col_place(sub, k)]
        side = core if mine else 1 - core
        return [jnp.dot(tile, hg[side, h, own_h, :], preferred_element_type=F32) for h in hs]

    wts = Ring(NY // 2, 2, wt_term, y_dev, vpart, vc, v_s, v_r, (vcs, vcr, vd_s, vd_r, sib_dev))

    def wt_send():
        wts.last(vfin, 0)
        for h in range(2):
            vcf[h] = vfin[0, h].astype(BF)
            remote(vcf.at[h], vcx.at[h], vx_s.at[h], vx_r.at[h], xh_dev).start()
        wts.last(vfin, 1)

    def wt_spread():
        for d in range(2):
            remote(vcx.at[d], vcx.at[d], vx_s.at[d], vx_r.at[d], xh_dev).wait_recv()
            value = (vfin[1, d] + vcx[d].astype(F32)).astype(BF)
            for k in range(NZ):
                ws[k, :, d * QUART:(d + 1) * QUART] = value[16 * k:16 * (k + 1), :]
        for k in range(1, NZ):
            remote(ws.at[(z + k) % NZ], wr.at[z], z_s, z_r.at[k], z_dev(k)).start()

    def wt_sum():
        total = ws[z].astype(F32)
        for k in range(1, NZ):
            zz = (z - k + NZ) % NZ
            remote(wr.at[zz], wr.at[zz], z_s, z_r.at[k], z_dev(k)).wait_recv()
            total = total + wr[zz].astype(F32)
        wxs[...] = total.astype(BF)
        remote(wxs, wxr, zx_s, zx_r, xl_dev).start()

    def wout_at(k, zz, side):
        lanes = pl.ds(pl.multiple_of(side * 512, 512), 512)
        return wout.at[k, zz, :, lanes]

    def wt_share():
        remote(wxr, wxr, zx_s, zx_r, xl_dev).wait_recv()
        value = (wxs[...].astype(F32) + wxr[...].astype(F32)).astype(BF)
        wfin[...] = value
        wout[chip, z, :, pl.ds(pl.multiple_of(core * 512, 512), 512)] = value
        for k in range(1, 8):
            remote(wfin, wout_at(chip, z, core), k_s, k_r.at[k], chip_dev(k)).start()

    def wz_at(k, side):
        lanes = pl.ds(pl.multiple_of(side * 512, 512), 512)
        return wout.at[:, (z + k + NZ) % NZ, :, lanes]

    def wz_send(d, s):
        here = wz_at((2 * d - 1) * s, core)
        if s < (NZ // 2 if d == 0 else NZ // 2 - 1):
            remote(here, here, g_s.at[d], g_r.at[d, s], z_dev(1 - 2 * d)).start()
        if s > 0 or d == 0:
            remote(here, here, gd_s, gd_r.at[d, s], sib_dev).start()

    def wz_start():
        for k in range(1, 8):
            there = wout_at((chip - k + 8) % 8, z, core)
            remote(there, there, k_s, k_r.at[k], chip_dev(k)).wait_recv()
        for d in range(2):
            wz_send(d, 0)

    def wz_step(s):
        for d in range(2):
            if s <= (NZ // 2 if d == 0 else NZ // 2 - 1):
                here = wz_at((2 * d - 1) * s, core)
                remote(here, here, g_s.at[d], g_r.at[d, s - 1], z_dev(1 - 2 * d)).wait_recv()
                wz_send(d, s)

    def wz_finish():
        for d in range(2):
            for s in range(NZ // 2 + 1 if d == 0 else NZ // 2):
                if s > 0 or d == 0:
                    here = wz_at((2 * d - 1) * s, 1 - core)
                    remote(here, here, gd_s, gd_r.at[d, s], sib_dev).wait_recv()

    def flip(lo, n):
        def one(t, carry):
            tiles_t[t] = tiles[t].T
            return carry
        lax.fori_loop(lo, lo + n, one, 0)

    ac_start(0)
    ac_start(1)
    loads[0].wait()
    tiles[64] = jnp.zeros((BLK, BLK), BF)
    tiles_t[64] = jnp.zeros((BLK, BLK), BF)
    ac_event(0, 0)
    ac_event(0, 1)
    ac_event(1, 0)
    ac_event(0, 2)
    ac_event(1, 1)
    ac_event(0, 3)
    ac_event(1, 2)
    ac_event(0, 4)
    ac_finish(0)
    row_a.own(0)
    row_a.step(0)
    ac_event(1, 3)
    row_a.own(1)
    ac_event(1, 4)
    ac_finish(1)
    loads[1].wait()
    loads[2].wait()
    row_b.other(0)
    row_b.other(1)
    row_b.own(0)
    row_a.step(1)
    row_b.step(0)
    flip(0, 20)
    for s in range(1, NZ // 2):
        if s < NZ // 2 - 1:
            row_a.own(s + 1)
            row_b.other(s + 1)
        else:
            row_a.last_own(fin.at[0])
            row_b.other(s + 1)
        row_b.own(s)
        if s < NZ // 2 - 1:
            row_a.step(s + 1)
        else:
            row_send()
        row_b.step(s)
        if s < NZ // 2 - 1:
            flip(20 * s, 20)
    row_b.last_own(fin.at[1])
    flip(60, 4)
    row_finish(0)
    row_b.last(fin.at[1], 0)
    row_finish(1)
    activate(0)
    ag_start(0)
    activate(1)
    act_store = pltpu.make_async_copy(act, act_out, store_sem.at[0])
    act_store.start()
    ag_start(1)
    ag_partner(0)
    turn_z()
    wts.other(0)
    wts.own(0)
    for s in range(1, NZ // 2 + 1):
        ag_step(0, 1, s)
        if s == 1:
            wts.step(0)
            wts.other(1)
            wts.own(1)
        if s == 2:
            wt_send()
        ag_step(1, 1, s)
        ag_step(0, 0, s)
        if s == 1:
            wts.step(1)
            wts.other(2)
            wts.last_own(vfin)
        if s == 2:
            wt_spread()
        if s == 3:
            wt_sum()
    wt_share()
    cols[0].other(0)
    cols[0].own(0)
    wz_start()
    ag_partner(1)
    cols[1].other(0)
    cols[1].own(0)
    cols[0].step(0)
    cols[0].other(1)
    cols[0].own(1)
    cols[1].step(0)
    wz_step(1)
    cols[1].other(1)
    cols[1].own(1)
    cols[0].step(1)
    cols[0].other(2)
    cols[0].last_own(fin.at[0])
    cols[1].step(1)
    wz_step(2)
    cols[1].other(2)
    cols[1].last_own(fin.at[1])
    col_send(0)
    wz_step(3)
    col_send(1)
    col_finish(0)
    wz_step(4)
    col_finish(1)
    fgrad_store = pltpu.make_async_copy(fgrad, fgrad_out, store_sem.at[1])
    fgrad_store.start()
    wz_finish()
    wout_store = pltpu.make_async_copy(wout, wout_out, store_sem.at[2])
    wout_store.start()
    fgrad_store.wait()
    wout_store.wait()
    act_store.wait()

    for p in range(2):
        for sub in range(2):
            for e in range(2):
                if (p == 0 or sub == 1):
                    sent = xg.at[0, 0, pl.ds(0, 3 * BLK)]
                    remote(sent, sent, a_ys.at[p, sub, e], a_yr.at[p, sub, 0], y_dev(e)).wait_send()
                if (p == 0 or sub == 1):
                    sent = hg.at[0, 0, pl.ds(0, 7 * BLK)]
                    remote(sent, sent, c_s.at[p, sub, e], c_r.at[p, sub, 0, 0], z_dev(1)).wait_send()
            sent = xg.at[0, 0, pl.ds(0, 8 * BLK)]
            remote(sent, sent, a_ds.at[p, sub], a_dr.at[p, sub, 0], sib_dev).wait_send()
        sent = xg.at[0, 0, pl.ds(0, (8 if p else 2) * BLK)]
        remote(sent, sent, a_xs.at[p], a_xr.at[p, 0], xh_dev).wait_send()
        for h in range(2):
            remote(rcx.at[p, h], rcx.at[p, h], ex_s.at[p, h], ex_r.at[p, h], xh_dev).wait_send()
        sent = hg.at[0, 0, pl.ds(0, (16 if p else 2) * BLK)]
        remote(sent, sent, cx_s.at[p], cx_r.at[p, 0], xl_dev).wait_send()
        cols[p].drain()
    row_a.drain()
    row_b.drain()
    for h in range(2):
        remote(rrx.at[h], rrx.at[h], bx_s.at[h], bx_r.at[h], xl_dev).wait_send()
    wts.drain()
    for h in range(2):
        remote(vcx.at[h], vcx.at[h], vx_s.at[h], vx_r.at[h], xh_dev).wait_send()
    sent = wr.at[pl.ds(0, 7)]
    remote(sent, sent, z_s, z_r.at[1], z_dev(1)).wait_send()
    sent = wr.at[pl.ds(0, 7)]
    remote(sent, sent, k_s, k_r.at[1], chip_dev(1)).wait_send()
    remote(wxs, wxs, zx_s, zx_r, xl_dev).wait_send()
    for d in range(2):
        sent = wout.at[:, pl.ds(0, NZ // 2 - d), :, pl.ds(0, 512)]
        remote(sent, sent, g_s.at[d], g_r.at[d, 0], z_dev(1)).wait_send()
    sent = wout.at[:, :, :, pl.ds(0, 512)]
    remote(sent, sent, gd_s, gd_r.at[0, 0], sib_dev).wait_send()


def layer(slot_of, features, weight, cotangent, tiles):
    hbm = pl.BlockSpec(memory_space=pl.ANY)
    dma = pltpu.SemaphoreType.DMA
    chunk = (BLK, QUART)
    return pl.pallas_call(
        kernel,
        name="layer",
        out_shape=(
            jax.ShapeDtypeStruct((BLK, 1024), BF),
            jax.ShapeDtypeStruct((BLK, 1024), BF),
            jax.ShapeDtypeStruct((8, NZ, 16, 1024), BF),
        ),
        in_specs=[pl.BlockSpec(memory_space=pltpu.SMEM)] + [hbm] * 4,
        out_specs=(hbm, hbm, hbm),
        scratch_shapes=[
            pltpu.VMEM((1024, 1024), BF),
            pltpu.VMEM((BLK, 1024), BF),
            pltpu.VMEM((BLK, 1024), BF),
            pltpu.VMEM((BLK, 1024), BF),
            pltpu.VMEM((8, NZ, 16, 1024), BF),
            pltpu.VMEM((2, 2, 2048, QUART), BF),
            pltpu.VMEM((2, 2, 2048, QUART), BF),
            pltpu.VMEM((65, BLK, BLK), BF),
            pltpu.VMEM((65, BLK, BLK), BF),
            pltpu.VMEM((BLK, 2048), BF),
            pltpu.VMEM((BLK, 1024), F32),
            pltpu.VMEM((4, *chunk), BF),
            pltpu.VMEM((8, BLK, BLK), BF),
            pltpu.VMEM((2, 4, 2, *chunk), F32),
            pltpu.VMEM((2, 2, 2, *chunk), F32),
            pltpu.VMEM((4, 2, 5, *chunk), BF),
            pltpu.VMEM((2, *chunk), BF),
            pltpu.VMEM((2, *chunk), BF),
            pltpu.VMEM((2, 2, 5, *chunk), BF),
            pltpu.VMEM((2, 2, 5, *chunk), BF),
            pltpu.VMEM((2, 2, 5, *chunk), BF),
            pltpu.VMEM((2, 4, 2, 3, *chunk), BF),
            pltpu.VMEM((2, 4, 2, 3, *chunk), BF),
            pltpu.VMEM((2, 4, 2, 3, *chunk), BF),
            pltpu.VMEM((2, 2, *chunk), BF),
            pltpu.VMEM((2, 2, *chunk), BF),
            pltpu.VMEM((4, 2, *chunk), F32),
            pltpu.VMEM((2, 2, *chunk), F32),
            pltpu.VMEM((4, 2, 3, *chunk), BF),
            pltpu.VMEM((4, 2, 3, *chunk), BF),
            pltpu.VMEM((4, 2, 3, *chunk), BF),
            pltpu.VMEM((2, *chunk), BF),
            pltpu.VMEM((2, *chunk), BF),
            pltpu.VMEM((NZ, 16, 512), BF),
            pltpu.VMEM((NZ, 16, 512), BF),
            pltpu.VMEM((16, 512), BF),
            pltpu.VMEM((16, 512), BF),
            pltpu.VMEM((16, 512), BF),
            dma((3,)), dma((2, 2)), dma((3,)),
            dma((2, 2, 2)), dma((2, 2, 6)), dma((2,)), dma((2, 8)), dma((2, 2)), dma((2, 2, 8)),
            dma((4,)), dma((4, 2, 4)), dma((2,)), dma((2,)), dma((2,)), dma((2, 2, 4)), dma((2,)), dma((2, 2, 5)),
            dma((2, 2, 2)), dma((2, 2, 4, 4)), dma((2,)), dma((2, 18)),
            dma((2, 4)), dma((2, 4, 2, 2)), dma((2, 2)), dma((2, 2)), dma((2, 4)), dma((2, 4, 2, 3)),
            dma((4,)), dma((4, 2, 2)), dma((2,)), dma((2,)), dma((4,)), dma((4, 2, 3)),
            dma, dma((NZ,)), dma, dma, dma, dma((NZ,)), dma((2,)), dma((2, 4)), dma, dma((2, 5)),
        ],
        compiler_params=pltpu.CompilerParams(
            collective_id=0, has_side_effects=True, vmem_limit_bytes=60 * 1024 * 1024,
        ),
    )(slot_of, features, weight, cotangent, tiles)


def on_device(features, weight, cotangent, tile_values, block_row, block_column, tile_count):
    slots = jnp.arange(64, dtype=jnp.int32)
    cells = jnp.arange(256, dtype=jnp.int32)[:, None]
    named = (block_row[0] == cells // 16) & (block_column[0] == cells % 16) & (slots < tile_count[0, 0])
    slot_of = jnp.min(jnp.where(named, slots, 64), axis=1)
    activated, feat_grad, pieces = layer(slot_of, features, weight, cotangent, tile_values[0, 0])
    weight_grad = pieces.reshape(1024, 1024).astype(F32) * 32768 ** (-0.5)
    return activated, feat_grad, weight_grad


def solution(mesh):
    return jax.shard_map(
        on_device,
        mesh=mesh,
        in_specs=(
            P(("row", "col"), None),
            P(),
            P(("col", "row"), None),
            P("row", "col", None, None, None),
            P("row", "col", None),
            P("row", "col", None),
            P("row", "col"),
        ),
        out_specs=(P(("col", "row"), None), P(("row", "col"), None), P()),
        check_vma=False,
    )
```

```python
import jax
import jax.numpy as jnp
from jax import lax
from jax.experimental import pallas as pl
from jax.experimental.pallas import tpu as pltpu
from jax.sharding import PartitionSpec as P

MESH = pl.DeviceIdType.MESH
BF = jnp.bfloat16
F32 = jnp.float32
NZ = 8
NY = 4
BLK = 128
QUART = 256


def remote(src, dst, send, recv, device):
    return pltpu.make_async_remote_copy(
        src_ref=src, dst_ref=dst, send_sem=send, recv_sem=recv,
        device_id=device, device_id_type=MESH,
    )


def kernel(
    slot_of, feat_in, weight_in, cot_in, tiles_in,
    act_out, fgrad_out, wout_out,
    weight, cot, act, fgrad, wout, xg, hg, tiles, tiles_t, strip, acc, zq, zt,
    part, fin, rr, rrs, rrx, rb, rbs, rbr, rc, rcs, rcr, rcf, rcx,
    vpart, vfin, vc, vcs, vcr, vcf, vcx, ws, wr, wxs, wxr, wfin,
    load_sem, feat_sem, store_sem,
    a_ys, a_yr, a_xs, a_xr, a_ds, a_dr,
    b_s, b_r, bx_s, bx_r, n_s, n_r, nx_s, nx_r,
    c_s, c_r, cx_s, cx_r,
    e_s, e_r, ex_s, ex_r, ed_s, ed_r,
    v_s, v_r, vx_s, vx_r, vd_s, vd_r,
    z_s, z_r, zx_s, zx_r, k_s, k_r, g_s, g_r, gd_s, gd_r,
):
    row = lax.axis_index("row")
    col = lax.axis_index("col")
    xl, z = row // NZ, row % NZ
    xh, y, core = col // 8, (col // 2) % NY, col % 2
    chip = xh * NY + y

    def z_dev(k):
        return (xl * NZ + (z + k + NZ) % NZ, col)

    def y_dev(d):
        return (row, xh * 8 + ((y + 1 - 2 * d + NY) % NY) * 2 + core)

    xl_dev = ((1 - xl) * NZ + z, col)
    xh_dev = (row, (1 - xh) * 8 + y * 2 + core)
    sib_dev = (row, xh * 8 + y * 2 + 1 - core)

    def chip_dev(k):
        other = (chip + k) % 8
        return (row, other * 2 + core)

    def feat_load(p, d):
        lanes = pl.ds((2 * p + d) * QUART, QUART)
        return pltpu.make_async_copy(
            feat_in.at[:, lanes], xg.at[p, d, pl.ds(pl.multiple_of(col * BLK, BLK), BLK)], feat_sem.at[p, d])

    loads = [
        pltpu.make_async_copy(tiles_in, tiles.at[pl.ds(0, 64)], load_sem.at[0]),
        pltpu.make_async_copy(weight_in, weight, load_sem.at[1]),
        pltpu.make_async_copy(cot_in, cot, load_sem.at[2]),
    ]
    barrier = pltpu.get_barrier_semaphore()
    peers = [chip_dev(k) for k in range(1, 8)] + [z_dev(k) for k in range(1, NZ)] + [xl_dev, sib_dev]
    for peer in peers:
        pl.semaphore_signal(barrier, inc=1, device_id=peer, device_id_type=MESH)
    for p in range(2):
        for d in range(2):
            feat_load(p, d).start()
    for load in loads:
        load.start()
    for p in range(2):
        for d in range(2):
            feat_load(p, d).wait()
    pl.semaphore_wait(barrier, len(peers))

    def xg_at(p, h, sub, k, other):
        xx = xh if sub == 1 else 1 - xh
        c = xx * 8 + ((y + k + NY) % NY) * 2 + (1 - core if other else core)
        return xg.at[p, h, pl.ds(pl.multiple_of(c * BLK, BLK), BLK)]

    def ac_places(s):
        return [(e, h) for e in range(2) for h in ((e, 1 - e) if s == 1 else (e,))]

    def ac_sem(e, h, s):
        return 2 * e + h if s == 1 else 4 + e

    def ac_send(p, sub, e, h, s):
        here = xg_at(p, h, sub, (2 * e - 1) * s, False)
        remote(here, here, a_ys.at[p, sub, e], a_yr.at[p, sub, ac_sem(e, h, s + 1)], y_dev(e)).start()

    def ac_cross(p, sub, h, k, i):
        here = xg_at(p, h, sub, k, False)
        remote(here, here, a_ds.at[p, sub], a_dr.at[p, sub, i], sib_dev).start()

    def ac_first(p, sub):
        for e, h in ac_places(1):
            ac_send(p, sub, e, h, 0)

    def ac_start(p):
        ac_first(p, 1)
        for h in range(2):
            ac_over(p, h, 0, h)
        for h in range(2):
            ac_cross(p, 1, h, 0, h)

    def ac_over(p, h, k, i):
        here = xg_at(p, h, 1, k, False)
        remote(here, here, a_xs.at[p], a_xr.at[p, i], xh_dev).start()

    def ac_over_wait(p, h, k, i):
        here = xg_at(p, h, 0, k, False)
        remote(here, here, a_xs.at[p], a_xr.at[p, i], xh_dev).wait_recv()

    def ac_event(p, i):
        sub, s = ((1, 1), (0, 0), (1, 2), (0, 1), (0, 2))[i]
        if s == 0:
            for h in range(2):
                ac_over_wait(p, h, 0, h)
            if p == 0:
                ac_first(p, 0)
            for h in range(2):
                ac_cross(p, 0, h, 0, h)
            return
        for e, h in ac_places(s):
            k = (2 * e - 1) * s
            i = 2 + ac_sem(e, h, s)
            if p == 1 and sub == 0:
                ac_over_wait(p, h, k, i)
            else:
                here = xg_at(p, h, sub, k, False)
                remote(here, here, a_ys.at[p, sub, e], a_yr.at[p, sub, i - 2], y_dev(e)).wait_recv()
                if s == 1 and h == e:
                    ac_send(p, sub, e, h, 1)
                if p == 1:
                    ac_over(p, h, k, i)
            ac_cross(p, sub, h, k, i)

    def ac_finish(p):
        for sub in (1, 0):
            for h in range(2):
                here = xg_at(p, h, sub, 0, True)
                remote(here, here, a_ds.at[p, sub], a_dr.at[p, sub, h], sib_dev).wait_recv()
            for s in (1, 2):
                for e, h in ac_places(s):
                    here = xg_at(p, h, sub, (2 * e - 1) * s, True)
                    remote(here, here, a_ds.at[p, sub], a_dr.at[p, sub, 2 + ac_sem(e, h, s)], sib_dev).wait_recv()

    def lay(table, first, step):
        for i in range(16):
            strip[:, i * BLK:(i + 1) * BLK] = table[slot_of[first + i * step]]

    def times(source):
        return jnp.dot(strip[...], source, preferred_element_type=F32)

    class Ring:
        def __init__(self, reach, subs, term, ring_dev, terms, held, send, recv, cross=None):
            self.reach, self.subs, self.term, self.ring_dev = reach, subs, term, ring_dev
            self.terms, self.held, self.send, self.recv, self.cross = terms, held, send, recv, cross

        def split(self, q, s):
            e, sub = q // self.subs, q % self.subs
            return e, sub, (1 - 2 * e) * (self.reach - s), ((e,) if s == 0 else (e, 1 - e))

        def other(self, s):
            out, into, send, recv, dev = self.cross

            def one(q, inner):
                e, sub, k, hs = self.split(q, s)
                for h, value in zip(hs, self.term(False, e, sub, k, hs)):
                    out[q, h, s] = value.astype(BF)
                    remote(out.at[q, h, s], into.at[q, h, s], send.at[q], recv.at[q, h, s], dev).start()
                return inner

            lax.fori_loop(0, 2 * self.subs if s < self.reach else self.subs, one, 0)

        def own(self, s):
            def one(q, inner):
                e, sub, k, hs = self.split(q, s)
                for h, value in zip(hs, self.term(True, e, sub, k, hs)):
                    self.terms[q, h] = value
                return inner

            lax.fori_loop(0, 2 * self.subs, one, 0)

        def add_cross(self, q, h, s):
            if self.cross is None:
                return 0.0
            into, send, recv, dev = self.cross[1:]
            remote(into.at[q, h, s], into.at[q, h, s], send.at[q], recv.at[q, h, s], dev).wait_recv()
            return into[q, h, s].astype(F32)

        def add_ring(self, e, q, h, s):
            here = self.held.at[q, h, s]
            remote(here, here, self.send.at[q], self.recv.at[q, h, s - 1], self.ring_dev(e)).wait_recv()
            return self.held[q, h, s].astype(F32)

        def step(self, s):
            def one(q, inner):
                e, sub, k, hs = self.split(q, s)
                for i, h in enumerate(hs):
                    value = self.terms[q, h] + self.add_cross(q, h, s)
                    if s > i:
                        value = value + self.add_ring(e, q, h, s)
                    self.held[q, h, s] = value.astype(BF)
                    remote(self.held.at[q, h, s], self.held.at[q, h, s + 1], self.send.at[q],
                           self.recv.at[q, h, s], self.ring_dev(e)).start()
                return inner

            lax.fori_loop(0, 2 * self.subs, one, 0)

        def last_own(self, sums):
            def one(sub, inner):
                for h, value in zip((0, 1), self.term(True, 0, sub, 0, (0, 1))):
                    sums[sub, h] = value
                return inner

            lax.fori_loop(0, self.subs, one, 0)

        def last(self, sums, sub):
            for h in range(2):
                value = sums[sub, h] + self.add_cross(sub, h, self.reach)
                for e in range(2):
                    value = value + self.add_ring(e, e * self.subs + sub, h, self.reach)
                sums[sub, h] = value

        def drain(self):
            for q in range(2 * self.subs):
                sent = xg.at[0, 0, pl.ds(0, (2 * self.reach - 1) * BLK)]
                remote(sent, sent, self.send.at[q], self.recv.at[q, 0, 0], self.ring_dev(0)).wait_send()
                if self.cross is not None:
                    send, recv, dev = self.cross[2:]
                    count = 2 * self.reach - 1 + (2 if q < self.subs else 0)
                    sent = xg.at[0, 0, pl.ds(0, count * BLK)]
                    remote(sent, sent, send.at[q], recv.at[q, 0, 0], dev).wait_send()

    def z_ring_dev(e):
        return z_dev(1 - 2 * e)

    def row_term_0(mine, e, sub, k, hs):
        xd = xl + (1 - sub) * (1 - 2 * xl)
        lay(tiles, (xd * NZ + (z + k + NZ) % NZ) * 16, 1)
        return [times(xg[0, h]) for h in hs]

    row_a = Ring(NZ // 2, 2, row_term_0, z_ring_dev, part.at[0], rr, b_s, b_r)

    def row_term_1(mine, e, sub, k, hs):
        lay(tiles, ((xl if mine else 1 - xl) * NZ + (z + k + NZ) % NZ) * 16, 1)
        return [times(xg[1, h]) for h in hs]

    row_b = Ring(NZ // 2, 1, row_term_1, z_ring_dev, part.at[1], rb, n_s, n_r, (rbs, rbr, nx_s, nx_r, xl_dev))

    def row_send():
        row_a.last(fin.at[0], 0)
        for h in range(2):
            rrs[h] = fin[0, 0, h].astype(BF)
            remote(rrs.at[h], rrx.at[h], bx_s.at[h], bx_r.at[h], xl_dev).start()
        row_a.last(fin.at[0], 1)

    def row_finish(p):
        for h in range(2):
            if p == 0:
                remote(rrx.at[h], rrx.at[h], bx_s.at[h], bx_r.at[h], xl_dev).wait_recv()
                zq[h] = (fin[0, 1, h] + rrx[h].astype(F32)).astype(BF)
            else:
                zq[2 + h] = fin[1, 0, h].astype(BF)
        both = jnp.concatenate([zq[2 * p], zq[2 * p + 1]], axis=1)
        value = jnp.dot(both, weight[pl.ds(p * 512, 512), :], preferred_element_type=F32)
        if p == 0:
            acc[...] = value
        else:
            acc[...] = acc[...] + value

    own_h = pl.ds(pl.multiple_of(row * BLK, BLK), BLK)

    def activate(p):
        for d in range(2):
            lanes = slice((2 * p + d) * QUART, (2 * p + d + 1) * QUART)
            hidden = acc[:, lanes]
            sig = 1.0 / (1.0 + jnp.exp(-hidden))
            act[:, lanes] = (hidden * sig).astype(BF)
            slope = sig * (1.0 + hidden * (1.0 - sig))
            hg[p, d, own_h, :] = (cot[:, lanes].astype(F32) * slope).astype(BF)

    def hg_at(p, h, sub, k):
        xx = xl if sub == 1 else 1 - xl
        return hg.at[p, h, pl.ds(pl.multiple_of((xx * NZ + (z + k + NZ) % NZ) * BLK, BLK), BLK)]

    def ag_places(s):
        return [(e, h) for e in range(2) for h in (e, 1 - e) if s <= NZ // 2 - (h != e)]

    def ag_send(p, sub, e, h, s):
        here = hg_at(p, h, sub, (2 * e - 1) * s)
        remote(here, here, c_s.at[p, sub, e], c_r.at[p, sub, 2 * e + h, s], z_ring_dev(e)).start()

    def ag_cross(p, h, k, i):
        here = hg_at(p, h, 1, k)
        remote(here, here, cx_s.at[p], cx_r.at[p, i], xl_dev).start()

    def ag_cross_wait(p, h, k, i):
        here = hg_at(p, h, 0, k)
        remote(here, here, cx_s.at[p], cx_r.at[p, i], xl_dev).wait_recv()

    def ag_start(p):
        for e, h in ag_places(1):
            ag_send(p, 1, e, h, 0)
        for h in range(2):
            ag_cross(p, h, 0, h)

    def ag_partner(p):
        for h in range(2):
            ag_cross_wait(p, h, 0, h)
        if p == 0:
            for e, h in ag_places(1):
                ag_send(p, 0, e, h, 0)
        else:
            for s in range(1, NZ // 2 + 1):
                for e, h in ag_places(s):
                    ag_cross_wait(p, h, (2 * e - 1) * s, 4 * s + 2 * e + h - 2)

    def ag_step(p, sub, s):
        for e, h in ag_places(s):
            k = (2 * e - 1) * s
            here = hg_at(p, h, sub, k)
            remote(here, here, c_s.at[p, sub, e], c_r.at[p, sub, 2 * e + h, s - 1], z_ring_dev(e)).wait_recv()
            if (e, h) in ag_places(s + 1):
                ag_send(p, sub, e, h, s)
            if p == 1:
                ag_cross(p, h, k, 4 * s + 2 * e + h - 2)

    def col_place(sub, k):
        return (xh + (1 - sub) * (1 - 2 * xh)) * NY + (y + k + NY) % NY

    def col_ring(p):
        def term(mine, e, sub, k, hs):
            lay(tiles_t, col_place(sub, k) * 2 + (core if mine else 1 - core), 16)
            return [times(hg[p, h]) for h in hs]

        return Ring(NY // 2, 2, term, y_dev, part.at[p], rc.at[p], e_s.at[p], e_r.at[p],
                    (rcs.at[p], rcr.at[p], ed_s.at[p], ed_r.at[p], sib_dev))

    cols = [col_ring(0), col_ring(1)]

    def col_send(p):
        cols[p].last(fin.at[p], 0)
        for h in range(2):
            rcf[p, h] = fin[p, 0, h].astype(BF)
            remote(rcf.at[p, h], rcx.at[p, h], ex_s.at[p, h], ex_r.at[p, h], xh_dev).start()
        cols[p].last(fin.at[p], 1)

    def col_finish(p):
        delta = []
        for h in range(2):
            remote(rcx.at[p, h], rcx.at[p, h], ex_s.at[p, h], ex_r.at[p, h], xh_dev).wait_recv()
            delta.append((fin[p, 1, h] + rcx[p, h].astype(F32)).astype(BF))
        value = lax.dot_general(
            jnp.concatenate(delta, axis=1), weight[:, pl.ds(p * 512, 512)],
            (((1,), (1,)), ((), ())), preferred_element_type=F32,
        )
        if p == 0:
            acc[...] = value
        else:
            fgrad[...] = (acc[...] + value).astype(BF)

    def turn_z():
        for k in range(8):
            zt[k] = zq[k // 2, :, (k % 2) * BLK:(k % 2 + 1) * BLK].T

    def wt_term(mine, e, sub, k, hs):
        tile = zt[col_place(sub, k)]
        side = core if mine else 1 - core
        return [jnp.dot(tile, hg[side, h, own_h, :], preferred_element_type=F32) for h in hs]

    wts = Ring(NY // 2, 2, wt_term, y_dev, vpart, vc, v_s, v_r, (vcs, vcr, vd_s, vd_r, sib_dev))

    def wt_send():
        wts.last(vfin, 0)
        for h in range(2):
            vcf[h] = vfin[0, h].astype(BF)
            remote(vcf.at[h], vcx.at[h], vx_s.at[h], vx_r.at[h], xh_dev).start()
        wts.last(vfin, 1)

    def wt_spread():
        for d in range(2):
            remote(vcx.at[d], vcx.at[d], vx_s.at[d], vx_r.at[d], xh_dev).wait_recv()
            value = (vfin[1, d] + vcx[d].astype(F32)).astype(BF)
            for k in range(NZ):
                ws[k, :, d * QUART:(d + 1) * QUART] = value[16 * k:16 * (k + 1), :]
        for k in range(1, NZ):
            remote(ws.at[(z + k) % NZ], wr.at[z], z_s, z_r.at[k], z_dev(k)).start()

    def wt_sum():
        total = ws[z].astype(F32)
        for k in range(1, NZ):
            zz = (z - k + NZ) % NZ
            remote(wr.at[zz], wr.at[zz], z_s, z_r.at[k], z_dev(k)).wait_recv()
            total = total + wr[zz].astype(F32)
        wxs[...] = total.astype(BF)
        remote(wxs, wxr, zx_s, zx_r, xl_dev).start()

    def wout_at(k, zz, side):
        lanes = pl.ds(pl.multiple_of(side * 512, 512), 512)
        return wout.at[k, zz, :, lanes]

    def wt_share():
        remote(wxr, wxr, zx_s, zx_r, xl_dev).wait_recv()
        value = (wxs[...].astype(F32) + wxr[...].astype(F32)).astype(BF)
        wfin[...] = value
        wout[chip, z, :, pl.ds(pl.multiple_of(core * 512, 512), 512)] = value
        for k in range(1, 8):
            remote(wfin, wout_at(chip, z, core), k_s, k_r.at[k], chip_dev(k)).start()

    def wz_at(k, side):
        lanes = pl.ds(pl.multiple_of(side * 512, 512), 512)
        return wout.at[:, (z + k + NZ) % NZ, :, lanes]

    def wz_send(d, s):
        here = wz_at((2 * d - 1) * s, core)
        if s < (NZ // 2 if d == 0 else NZ // 2 - 1):
            remote(here, here, g_s.at[d], g_r.at[d, s], z_dev(1 - 2 * d)).start()
        if s > 0 or d == 0:
            remote(here, here, gd_s, gd_r.at[d, s], sib_dev).start()

    def wz_start():
        for k in range(1, 8):
            there = wout_at((chip - k + 8) % 8, z, core)
            remote(there, there, k_s, k_r.at[k], chip_dev(k)).wait_recv()
        for d in range(2):
            wz_send(d, 0)

    def wz_step(s):
        for d in range(2):
            if s <= (NZ // 2 if d == 0 else NZ // 2 - 1):
                here = wz_at((2 * d - 1) * s, core)
                remote(here, here, g_s.at[d], g_r.at[d, s - 1], z_dev(1 - 2 * d)).wait_recv()
                wz_send(d, s)

    def wz_finish():
        for d in range(2):
            for s in range(NZ // 2 + 1 if d == 0 else NZ // 2):
                if s > 0 or d == 0:
                    here = wz_at((2 * d - 1) * s, 1 - core)
                    remote(here, here, gd_s, gd_r.at[d, s], sib_dev).wait_recv()

    def flip(lo, n):
        def one(t, carry):
            tiles_t[t] = tiles[t].T
            return carry
        lax.fori_loop(lo, lo + n, one, 0)

    ac_start(0)
    ac_start(1)
    loads[0].wait()
    tiles[64] = jnp.zeros((BLK, BLK), BF)
    tiles_t[64] = jnp.zeros((BLK, BLK), BF)
    ac_event(0, 0)
    ac_event(0, 1)
    ac_event(1, 0)
    ac_event(0, 2)
    ac_event(1, 1)
    ac_event(0, 3)
    ac_event(1, 2)
    ac_event(0, 4)
    ac_finish(0)
    row_a.own(0)
    row_a.step(0)
    ac_event(1, 3)
    row_a.own(1)
    ac_event(1, 4)
    ac_finish(1)
    loads[1].wait()
    loads[2].wait()
    row_b.other(0)
    row_b.other(1)
    row_b.own(0)
    row_a.step(1)
    row_b.step(0)
    flip(0, 20)
    for s in range(1, NZ // 2):
        if s < NZ // 2 - 1:
            row_a.own(s + 1)
            row_b.other(s + 1)
        else:
            row_a.last_own(fin.at[0])
            row_b.other(s + 1)
        row_b.own(s)
        if s < NZ // 2 - 1:
            row_a.step(s + 1)
        else:
            row_send()
        row_b.step(s)
        if s < NZ // 2 - 1:
            flip(20 * s, 20)
    row_b.last_own(fin.at[1])
    flip(60, 4)
    row_finish(0)
    row_b.last(fin.at[1], 0)
    row_finish(1)
    activate(0)
    ag_start(0)
    activate(1)
    act_store = pltpu.make_async_copy(act, act_out, store_sem.at[0])
    act_store.start()
    ag_start(1)
    ag_partner(0)
    turn_z()
    wts.other(0)
    wts.own(0)
    for s in range(1, NZ // 2 + 1):
        ag_step(0, 1, s)
        if s == 1:
            wts.step(0)
            wts.other(1)
            wts.own(1)
        if s == 2:
            wt_send()
        ag_step(1, 1, s)
        ag_step(0, 0, s)
        if s == 1:
            wts.step(1)
            wts.other(2)
            wts.last_own(vfin)
        if s == 2:
            wt_spread()
        if s == 3:
            wt_sum()
    wt_share()
    cols[0].other(0)
    cols[0].own(0)
    wz_start()
    ag_partner(1)
    cols[1].other(0)
    cols[1].own(0)
    cols[0].step(0)
    cols[0].other(1)
    cols[0].own(1)
    cols[1].step(0)
    wz_step(1)
    cols[1].other(1)
    cols[1].own(1)
    cols[0].step(1)
    cols[0].other(2)
    cols[0].last_own(fin.at[0])
    cols[1].step(1)
    wz_step(2)
    cols[1].other(2)
    cols[1].last_own(fin.at[1])
    col_send(0)
    wz_step(3)
    col_send(1)
    col_finish(0)
    wz_step(4)
    wz_finish()
    wout_store = pltpu.make_async_copy(wout, wout_out, store_sem.at[2])
    wout_store.start()
    col_finish(1)
    fgrad_store = pltpu.make_async_copy(fgrad, fgrad_out, store_sem.at[1])
    fgrad_store.start()
    fgrad_store.wait()
    wout_store.wait()
    act_store.wait()

    for p in range(2):
        for sub in range(2):
            for e in range(2):
                if (p == 0 or sub == 1):
                    sent = xg.at[0, 0, pl.ds(0, 3 * BLK)]
                    remote(sent, sent, a_ys.at[p, sub, e], a_yr.at[p, sub, 0], y_dev(e)).wait_send()
                if (p == 0 or sub == 1):
                    sent = hg.at[0, 0, pl.ds(0, 7 * BLK)]
                    remote(sent, sent, c_s.at[p, sub, e], c_r.at[p, sub, 0, 0], z_dev(1)).wait_send()
            sent = xg.at[0, 0, pl.ds(0, 8 * BLK)]
            remote(sent, sent, a_ds.at[p, sub], a_dr.at[p, sub, 0], sib_dev).wait_send()
        sent = xg.at[0, 0, pl.ds(0, (8 if p else 2) * BLK)]
        remote(sent, sent, a_xs.at[p], a_xr.at[p, 0], xh_dev).wait_send()
        for h in range(2):
            remote(rcx.at[p, h], rcx.at[p, h], ex_s.at[p, h], ex_r.at[p, h], xh_dev).wait_send()
        sent = hg.at[0, 0, pl.ds(0, (16 if p else 2) * BLK)]
        remote(sent, sent, cx_s.at[p], cx_r.at[p, 0], xl_dev).wait_send()
        cols[p].drain()
    row_a.drain()
    row_b.drain()
    for h in range(2):
        remote(rrx.at[h], rrx.at[h], bx_s.at[h], bx_r.at[h], xl_dev).wait_send()
    wts.drain()
    for h in range(2):
        remote(vcx.at[h], vcx.at[h], vx_s.at[h], vx_r.at[h], xh_dev).wait_send()
    sent = wr.at[pl.ds(0, 7)]
    remote(sent, sent, z_s, z_r.at[1], z_dev(1)).wait_send()
    sent = wr.at[pl.ds(0, 7)]
    remote(sent, sent, k_s, k_r.at[1], chip_dev(1)).wait_send()
    remote(wxs, wxs, zx_s, zx_r, xl_dev).wait_send()
    for d in range(2):
        sent = wout.at[:, pl.ds(0, NZ // 2 - d), :, pl.ds(0, 512)]
        remote(sent, sent, g_s.at[d], g_r.at[d, 0], z_dev(1)).wait_send()
    sent = wout.at[:, :, :, pl.ds(0, 512)]
    remote(sent, sent, gd_s, gd_r.at[0, 0], sib_dev).wait_send()


def layer(slot_of, features, weight, cotangent, tiles):
    hbm = pl.BlockSpec(memory_space=pl.ANY)
    dma = pltpu.SemaphoreType.DMA
    chunk = (BLK, QUART)
    return pl.pallas_call(
        kernel,
        name="layer",
        out_shape=(
            jax.ShapeDtypeStruct((BLK, 1024), BF),
            jax.ShapeDtypeStruct((BLK, 1024), BF),
            jax.ShapeDtypeStruct((8, NZ, 16, 1024), BF),
        ),
        in_specs=[pl.BlockSpec(memory_space=pltpu.SMEM)] + [hbm] * 4,
        out_specs=(hbm, hbm, hbm),
        scratch_shapes=[
            pltpu.VMEM((1024, 1024), BF),
            pltpu.VMEM((BLK, 1024), BF),
            pltpu.VMEM((BLK, 1024), BF),
            pltpu.VMEM((BLK, 1024), BF),
            pltpu.VMEM((8, NZ, 16, 1024), BF),
            pltpu.VMEM((2, 2, 2048, QUART), BF),
            pltpu.VMEM((2, 2, 2048, QUART), BF),
            pltpu.VMEM((65, BLK, BLK), BF),
            pltpu.VMEM((65, BLK, BLK), BF),
            pltpu.VMEM((BLK, 2048), BF),
            pltpu.VMEM((BLK, 1024), F32),
            pltpu.VMEM((4, *chunk), BF),
            pltpu.VMEM((8, BLK, BLK), BF),
            pltpu.VMEM((2, 4, 2, *chunk), F32),
            pltpu.VMEM((2, 2, 2, *chunk), F32),
            pltpu.VMEM((4, 2, 5, *chunk), BF),
            pltpu.VMEM((2, *chunk), BF),
            pltpu.VMEM((2, *chunk), BF),
            pltpu.VMEM((2, 2, 5, *chunk), BF),
            pltpu.VMEM((2, 2, 5, *chunk), BF),
            pltpu.VMEM((2, 2, 5, *chunk), BF),
            pltpu.VMEM((2, 4, 2, 3, *chunk), BF),
            pltpu.VMEM((2, 4, 2, 3, *chunk), BF),
            pltpu.VMEM((2, 4, 2, 3, *chunk), BF),
            pltpu.VMEM((2, 2, *chunk), BF),
            pltpu.VMEM((2, 2, *chunk), BF),
            pltpu.VMEM((4, 2, *chunk), F32),
            pltpu.VMEM((2, 2, *chunk), F32),
            pltpu.VMEM((4, 2, 3, *chunk), BF),
            pltpu.VMEM((4, 2, 3, *chunk), BF),
            pltpu.VMEM((4, 2, 3, *chunk), BF),
            pltpu.VMEM((2, *chunk), BF),
            pltpu.VMEM((2, *chunk), BF),
            pltpu.VMEM((NZ, 16, 512), BF),
            pltpu.VMEM((NZ, 16, 512), BF),
            pltpu.VMEM((16, 512), BF),
            pltpu.VMEM((16, 512), BF),
            pltpu.VMEM((16, 512), BF),
            dma((3,)), dma((2, 2)), dma((3,)),
            dma((2, 2, 2)), dma((2, 2, 6)), dma((2,)), dma((2, 8)), dma((2, 2)), dma((2, 2, 8)),
            dma((4,)), dma((4, 2, 4)), dma((2,)), dma((2,)), dma((2,)), dma((2, 2, 4)), dma((2,)), dma((2, 2, 5)),
            dma((2, 2, 2)), dma((2, 2, 4, 4)), dma((2,)), dma((2, 18)),
            dma((2, 4)), dma((2, 4, 2, 2)), dma((2, 2)), dma((2, 2)), dma((2, 4)), dma((2, 4, 2, 3)),
            dma((4,)), dma((4, 2, 2)), dma((2,)), dma((2,)), dma((4,)), dma((4, 2, 3)),
            dma, dma((NZ,)), dma, dma, dma, dma((NZ,)), dma((2,)), dma((2, 4)), dma, dma((2, 5)),
        ],
        compiler_params=pltpu.CompilerParams(
            collective_id=0, has_side_effects=True, vmem_limit_bytes=60 * 1024 * 1024,
        ),
    )(slot_of, features, weight, cotangent, tiles)


def on_device(features, weight, cotangent, tile_values, block_row, block_column, tile_count):
    slots = jnp.arange(64, dtype=jnp.int32)
    cells = jnp.arange(256, dtype=jnp.int32)[:, None]
    named = (block_row[0] == cells // 16) & (block_column[0] == cells % 16) & (slots < tile_count[0, 0])
    slot_of = jnp.min(jnp.where(named, slots, 64), axis=1)
    activated, feat_grad, pieces = layer(slot_of, features, weight, cotangent, tile_values[0, 0])
    weight_grad = pieces.reshape(1024, 1024).astype(F32) * 32768 ** (-0.5)
    return activated, feat_grad, weight_grad


def solution(mesh):
    return jax.shard_map(
        on_device,
        mesh=mesh,
        in_specs=(
            P(("row", "col"), None),
            P(),
            P(("col", "row"), None),
            P("row", "col", None, None, None),
            P("row", "col", None),
            P("row", "col", None),
            P("row", "col"),
        ),
        out_specs=(P(("col", "row"), None), P(("row", "col"), None), P()),
        check_vma=False,
    )
```
